32 devices in a mesh: replica: 2 (over x), fsdp: 4 (over z), tensor: 4 (over y, core).
Axes of the slice: x: 2, y: 2, z: 4, core: 2. Of those that a mesh axis runs over, the one named last changes fastest.
Arguments:
- tokens: bfloat16 [2, 2048, 2048], P('replica', ('fsdp', 'tensor')), may hold values from -6 to 6
- segments: int32 [2, 2048], P('replica'), may hold values from 0 to 7, never falling along the last dimension, each value on 1 to 1024 neighbouring positions
- w_qkv: bfloat16 [2, 3, 2048, 2048], P(None, None, 'fsdp', 'tensor'), may hold values from -0.1875 to 0.1875
- b_qkv: bfloat16 [2, 3, 32, 64], P(None, None, 'tensor', 'fsdp'), may hold values from -3 to 3
- w_out: bfloat16 [2, 2048, 2048], P(None, 'tensor', 'fsdp'), may hold values from -0.75 to 0.75
- w_gate_up: bfloat16 [2, 2, 2048, 5632], P(None, None, 'fsdp', 'tensor'), may hold values from -0.125 to 0.125
- w_down: bfloat16 [2, 5632, 2048], P(None, 'tensor', 'fsdp'), may hold values from -0.078125 to 0.078125
- ln_gain: bfloat16 [2, 2, 2048], P(None, None, ('fsdp', 'tensor')), may hold values from 0.5 to 1.5
- ln_bias: bfloat16 [2, 2, 2048], P(None, None, ('fsdp', 'tensor')), may hold values from -2 to 2
- cotangent: bfloat16 [2, 2048, 2048], P('replica', ('fsdp', 'tensor')), may hold values from -6 to 6
Outputs:
- output: bfloat16 [2, 2048, 2048], P('replica', ('fsdp', 'tensor'))
- input_grad: float32 [2, 2048, 2048], P('replica', ('fsdp', 'tensor'))
- grad_w_qkv: float32 [2, 3, 2048, 2048], P(None, None, 'fsdp', 'tensor')
- grad_b_qkv: float32 [2, 3, 32, 64], P(None, None, 'tensor', 'fsdp')
- grad_w_out: float32 [2, 2048, 2048], P(None, 'tensor', 'fsdp')
- grad_w_gate_up: float32 [2, 2, 2048, 5632], P(None, None, 'fsdp', 'tensor')
- grad_w_down: float32 [2, 5632, 2048], P(None, 'tensor', 'fsdp')
- grad_ln_gain: float32 [2, 2, 2048], P(None, None, ('fsdp', 'tensor'))
- grad_ln_bias: float32 [2, 2, 2048], P(None, None, ('fsdp', 'tensor'))
The draws below stay inside these ranges and needn't reach their ends.
Inputs may be any that keep to these rules, and one draw needn't show every extreme that they name: `segments`: segment numbers never fall along a sequence; each document holds 1 to 1024 tokens and one holds exactly 1024.
All inputs are finite; a program needn't handle non-finite values.
Results may differ from the reference program's by a relative error of at most 0.04.
Values may be sent and summed in bfloat16 or wider, within the bound.
No kernel may reach another device: no remote copies, remote signals or barrier semaphores. Data moves between devices by JAX's collectives and lax.ppermute only.
A program may use at most 320 MiB of HBM per device.

```python
import math
import jax
import jax.numpy as jnp
import numpy as np
from jax import lax

D = 2048
H = 32
HD = 64
FF = 5632
LAYERS = 2
ROT = 16
LEN = 2048
N_SEQ = 2


def level_of(rng, dims, shards, smallest, top_value):
    loudness, own = 1.0, jax.random.fold_in(rng, 6)
    for dim, parts in shards:
        draws = jnp.exp(jax.random.uniform(jax.random.fold_in(own, dim), (parts,), jnp.float32, smallest / len(shards), top_value / len(shards)))
        loudness = loudness * jnp.repeat(draws, dims[dim] // parts).reshape([-1 if axis == dim else 1 for axis in range(len(dims))])
    return loudness


def length_profile(count, total, bound, skew):
    loads = [(1 << 20) // math.isqrt(rank ** skew) + 1 for rank in range(2, count + 1)]
    spare, holding = total - bound - (count - 1), [1] * (count - 1)
    while spare > 0:
        movable = [i for i in range(count - 1) if holding[i] < bound]
        mass, budget = sum([loads[i] for i in movable]), spare
        for i in movable:
            addition = min(bound - holding[i], max(1, budget * loads[i] // mass), spare)
            holding[i] = holding[i] + addition
            spare = spare - addition
    return np.array([bound] + holding)


def uneven(rng, count, total, bound, lean):
    if count == 2:
        one = jax.random.randint(rng, (), max(1, total - bound), min(bound, total - 1) + 1)
        return jnp.stack([one, total - one])
    tallies = jnp.asarray(length_profile(count, total, bound, lean), jnp.int32)
    pairs = (count - 1) // 2
    donor, taker = tallies[1:1 + 2 * pairs:2], tallies[2:2 + 2 * pairs:2]
    slack = jnp.minimum(donor - 1, bound - taker)
    shifted = jax.random.randint(jax.random.fold_in(rng, 1), (pairs,), 0, 1 << 20) % (slack + 1)
    tallies = tallies.at[1:1 + 2 * pairs:2].set(donor - shifted).at[2:2 + 2 * pairs:2].set(taker + shifted)
    return tallies[jax.random.permutation(jax.random.fold_in(rng, 2), count)]


def gaussian(own_key, shape, deviation, bound, shards=(), kind=jnp.bfloat16):
    loudness = level_of(own_key, shape, shards, -0.22, 0.18) if shards else 1.0
    array = jax.random.normal(own_key, shape, jnp.float32) * deviation * loudness
    return jnp.minimum(jnp.maximum(array, -bound), bound).astype(kind)


def setup_inputs(seed: int = 0) -> dict:
    streams_of = jax.random.split(jax.random.key(seed), 11)
    return {
        "tokens": gaussian(streams_of[0], (N_SEQ, LEN, D), 1.0, 6.0, ((0, 2), (1, 16))),
        "segments": jax.vmap(lambda own: jnp.searchsorted(jnp.cumsum(uneven(own, max(LEN // 256, 4), LEN, LEN // 2, 0)), jnp.arange(LEN), side="right"))(jax.random.split(streams_of[1], N_SEQ)).reshape((N_SEQ, LEN)).astype(jnp.int32),
        "w_qkv": gaussian(streams_of[2], (LAYERS, 3, D, H * HD), (D // 2) ** -0.5, 0.1875, ((2, 4), (3, 4))),
        "b_qkv": gaussian(streams_of[3], (LAYERS, 3, H, HD), 0.5, 3.0, ((2, 4), (3, 4))),
        "w_out": gaussian(streams_of[4], (LAYERS, H * HD, D), HD ** -0.5, 0.75, ((1, 4), (2, 4))),
        "w_gate_up": gaussian(streams_of[5], (LAYERS, 2, D, FF), D ** -0.5, 0.125, ((2, 4), (3, 4))),
        "w_down": gaussian(streams_of[6], (LAYERS, FF, D), FF ** -0.5, 0.078125, ((1, 4), (2, 4))),
        "ln_gain": jnp.clip(1.0 + 0.1 * jax.random.normal(streams_of[7], (LAYERS, 2, D), jnp.float32), 0.5, 1.5).astype(jnp.bfloat16),
        "ln_bias": gaussian(streams_of[8], (LAYERS, 2, D), 0.3, 2.0, ((2, 16),)),
        "cotangent": gaussian(streams_of[9], (N_SEQ, LEN, D), 1.0, 6.0, ((0, 2), (1, 16))),
    }


@jax.custom_vjp
def low(v):
    return lax.optimization_barrier(v.astype(jnp.bfloat16)).astype(jnp.float32)

@jax.custom_vjp
def low_back(v):
    return v

def low_keep(v):
    return (low(v), None)

def low_pass(kept, grad):
    return (grad,)

def back_keep(v):
    return (v, None)

def back_low(kept, grad):
    return (low(grad),)
low.defvjp(low_keep, low_pass)
low_back.defvjp(back_keep, back_low)
EPSILON = 1e-05
PRECISE = lax.Precision.HIGHEST
MASKED = -1e+30

def positions_of(segment_row):
    index = jnp.arange(segment_row.shape[0], dtype=jnp.int32)
    earlier = jnp.concatenate([segment_row[:1] - 1, segment_row[:-1]])
    boundary = jnp.where(segment_row != earlier, index, jnp.zeros_like(index))
    return index - lax.cummax(boundary, axis=0)

def rotary_tables(positions):
    half_width = ROT // 2
    frequency = jnp.exp(-jnp.log(10000.0) * jnp.arange(half_width, dtype=jnp.float32) * 2.0 / ROT)
    angles = positions.astype(jnp.float32)[:, None] * frequency[None, :]
    return (jnp.cos(angles), jnp.sin(angles))

def rotate(heads_in, cosine, sine_table):
    half_width = ROT // 2
    lower_half = heads_in[..., :half_width]
    upper_half = heads_in[..., half_width:ROT]
    cos_part = cosine[:, None, :]
    sin_part = sine_table[:, None, :]
    return jnp.concatenate([lower_half * cos_part - upper_half * sin_part, upper_half * cos_part + lower_half * sin_part, heads_in[..., ROT:]], axis=-1)

def layer_norm(stream, gain_row, shift_row):
    average = lax.optimization_barrier(jnp.mean(stream, axis=-1, keepdims=True))
    centred = stream - average
    variance = lax.optimization_barrier(jnp.mean(centred * centred, axis=-1, keepdims=True))
    return centred * lax.rsqrt(variance + EPSILON) * gain_row + shift_row

def attend(query_all, key_all, value_all, segment_row):
    length = query_all.shape[0]
    block_size = min(512, length)
    index = jnp.arange(length, dtype=jnp.int32)
    scale = HD ** (-0.5)

    def one_block(anchor):
        query_part = lax.dynamic_slice_in_dim(query_all, anchor, block_size, 0)
        query_index = lax.dynamic_slice_in_dim(index, anchor, block_size, 0)
        query_segment = lax.dynamic_slice_in_dim(segment_row, anchor, block_size, 0)
        scores = low_back(jnp.einsum('qhd,khd->hqk', query_part, key_all, precision=PRECISE) * scale)
        allowed = (index[None, :] <= query_index[:, None]) & (segment_row[None, :] == query_segment[:, None])
        scores = jnp.where(allowed[None], scores, MASKED)
        probability = jax.nn.softmax(scores, axis=-1)
        return jnp.einsum('hqk,khd->qhd', low(probability), value_all, precision=PRECISE)
    anchors = jnp.arange(0, length, block_size, dtype=jnp.int32)
    result = lax.map(jax.checkpoint(one_block), anchors)
    return result.reshape(length, H * HD)

def layer(stream, segment_row, cosine, sine_table, params):
    w_qkv, b_qkv, w_out, w_gate_up, w_down, ln_gain, ln_bias = params
    length = stream.shape[0]
    normed = low(layer_norm(stream, ln_gain[0], ln_bias[0]))
    mixed = jnp.einsum('td,cde->cte', normed, w_qkv, precision=PRECISE) + b_qkv.reshape(3, 1, H * HD)
    mixed = low_back(mixed).reshape(3, length, H, HD)
    query_all = low_back(low(rotate(mixed[0], cosine, sine_table)))
    key_all = low_back(low(rotate(mixed[1], cosine, sine_table)))
    value_all = low_back(low(mixed[2]))
    attended = low_back(low(attend(query_all, key_all, value_all, segment_row)))
    stream_h = stream + low_back(jnp.dot(attended, w_out, precision=PRECISE))
    normed_two = low(layer_norm(stream_h, ln_gain[1], ln_bias[1]))
    gate_up = low_back(jnp.einsum('td,cdf->ctf', normed_two, w_gate_up, precision=PRECISE))
    activated = low(jax.nn.silu(gate_up[0]) * gate_up[1])
    return stream_h + low_back(jnp.dot(activated, w_down, precision=PRECISE))

def sequence_forward(stream, segment_row, params):
    cosine, sine_table = rotary_tables(positions_of(segment_row))
    for layer_index in range(LAYERS):
        stream = layer(stream, segment_row, cosine, sine_table, tuple((p[layer_index] for p in params)))
    return stream

def reference(tokens, segments, w_qkv, b_qkv, w_out, w_gate_up, w_down, ln_gain, ln_bias, cotangent):
    params = tuple((p.astype(jnp.float32) for p in (w_qkv, b_qkv, w_out, w_gate_up, w_down, ln_gain, ln_bias)))

    def one_sequence(grad_sum, scan_items):
        stream, segment_row, seed_grad = scan_items

        def forward(inputs, weights):
            return sequence_forward(inputs, segment_row, weights)
        result, pullback = jax.vjp(forward, stream.astype(jnp.float32), params)
        stream_grad, weight_grads = pullback(seed_grad.astype(jnp.float32))
        return (jax.tree.map(jnp.add, grad_sum, weight_grads), (result.astype(jnp.bfloat16), stream_grad))
    zero_grads = jax.tree.map(jnp.zeros_like, params)
    grads, (outputs, input_grads) = lax.scan(one_sequence, zero_grads, (tokens, segments, cotangent))
    return (outputs, input_grads, grads[0], grads[1], grads[2], grads[3], grads[4], grads[5], grads[6])
```

```python
import jax
import jax.numpy as jnp
from jax import lax
from jax.sharding import PartitionSpec as P

HD = 64
ROT = 16
EPSILON = 1e-05
MASKED = -1e30
LANES = 128
F32 = jnp.float32
BF16 = jnp.bfloat16


def pair_size():
    return 2 if lax.axis_size("replica") % 2 == 0 else 1


def swap_tensor(values, bit):
    count = lax.axis_size("tensor")
    return lax.ppermute(values, "tensor", [(i, i ^ bit) for i in range(count)])


def swap_replica(values):
    count = lax.axis_size("replica")
    return lax.ppermute(values, "replica", [(i, i ^ 1) for i in range(count)])


def shift_fsdp(values, step):
    count = lax.axis_size("fsdp")
    return lax.ppermute(
        values, "fsdp", [(i, i + step) for i in range(count) if 0 <= i + step < count]
    )


def gather_rows(rows):
    half = rows.shape[0] // 2
    a_own, b_own = rows[:half], rows[half:]
    a_y = swap_tensor(a_own, 2)
    b_x = swap_replica(b_own)
    a_pair = jnp.concatenate([a_own, a_y], 0)
    b_pair = jnp.concatenate([b_own, b_x], 0)
    a_x = swap_replica(a_pair)
    b_y = swap_tensor(b_pair, 2)
    mine = jnp.concatenate([a_pair, a_x, b_own, b_y[:half], b_x, b_y[half:]], 0)
    other = swap_tensor(mine, 1)
    return jnp.concatenate([mine, other], 0)


def add_low(first, second):
    return (first.astype(F32) + second.astype(F32)).astype(BF16)


def scatter_rows(partial):
    total, width = partial.shape
    half = total // 16
    received = swap_tensor(partial[total // 2 :], 1)
    mine = add_low(partial[: total // 2], received).reshape(2, 2, 2, half, width)
    a_part, b_part = mine[0], mine[1]
    a_in = swap_replica(a_part[1])
    b_in = swap_tensor(b_part[:, 1], 2)
    a_part = add_low(a_part[0], a_in)
    b_part = add_low(b_part[:, 0], b_in)
    a_in = swap_tensor(a_part[1], 2)
    b_in = swap_replica(b_part[1])
    a_row = a_part[0].astype(F32) + a_in.astype(F32)
    b_row = b_part[0].astype(F32) + b_in.astype(F32)
    return jnp.concatenate([a_row, b_row], 0)


def order_rows(blocks, own):
    picked = [
        [lax.dynamic_index_in_dim(blocks, own ^ (2 * y + c), 1, keepdims=False) for y in range(2)]
        for c in range(2)
    ]
    stacked = jnp.stack([jnp.stack(row) for row in picked])
    return jnp.transpose(stacked, (0, 3, 2, 1, 4)).reshape(-1)


def segment_starts(segment_rows):
    length = segment_rows.shape[1]
    index = jnp.arange(length, dtype=jnp.int32)
    earlier = jnp.concatenate([segment_rows[:, :1] - 1, segment_rows[:, :-1]], 1)
    boundary = jnp.where(segment_rows != earlier, index[None, :], 0)
    return lax.cummax(boundary, axis=1)


def rotary_tables(positions):
    half_width = ROT // 2
    frequency = jnp.exp(-jnp.log(10000.0) * jnp.arange(half_width, dtype=F32) * 2.0 / ROT)
    angles = positions.astype(F32)[:, None] * frequency[None, :]
    return (jnp.cos(angles), jnp.sin(angles))


def rotate(heads_in, cosine, sine_table):
    half_width = ROT // 2
    lower_half = heads_in[..., :half_width]
    upper_half = heads_in[..., half_width:ROT]
    cos_part = cosine[:, None, :]
    sin_part = sine_table[:, None, :]
    return jnp.concatenate(
        [
            lower_half * cos_part - upper_half * sin_part,
            upper_half * cos_part + lower_half * sin_part,
            heads_in[..., ROT:],
        ],
        axis=-1,
    )


def norm_forward(stream, gain_row, shift_row):
    average = jnp.mean(stream, axis=-1, keepdims=True)
    centred = stream - average
    variance = jnp.mean(centred * centred, axis=-1, keepdims=True)
    reciprocal = lax.rsqrt(variance + EPSILON)
    scaled = centred * reciprocal
    return (scaled * gain_row + shift_row, scaled, reciprocal)


def norm_backward(gradient, scaled, reciprocal, gain_row):
    weighted_grad = gradient * gain_row
    result = reciprocal * (
        weighted_grad
        - jnp.mean(weighted_grad, axis=-1, keepdims=True)
        - scaled * jnp.mean(weighted_grad * scaled, axis=-1, keepdims=True)
    )
    return (result, jnp.sum(gradient * scaled, axis=0), jnp.sum(gradient, axis=0))


def by_sequence(values, heads):
    rows = values.shape[0]
    split = values.reshape(4, 2, rows // 8, heads, HD)
    return jnp.transpose(split, (1, 0, 2, 3, 4)).reshape(2, rows // 2, heads, HD)


def by_row(values):
    _, rows, heads, width = values.shape
    split = values.reshape(2, 4, rows // 4, heads * width)
    return jnp.transpose(split, (1, 0, 2, 3)).reshape(2 * rows, heads * width)


def key_blocks(packed, heads):
    before = shift_fsdp(packed, 1)
    earlier = shift_fsdp(before, 1)
    joined = jnp.stack([packed, before, earlier])
    return joined


def allowed_mask(context, step):
    query_index, query_start, row_count = context
    key_index = query_index - step * row_count
    return (key_index[:, None, :] <= query_index[:, :, None]) & (
        key_index[:, None, :] >= query_start[:, :, None]
    )


def attend(query, keys, values, context):
    scores = []
    for step in range(3):
        raw = (
            jnp.einsum("sqhd,skhd->shqk", query, keys[step], preferred_element_type=F32)
            * HD ** (-0.5)
        )
        scores.append(jnp.where(allowed_mask(context, step)[:, None], raw, MASKED))
    top = jnp.maximum(jnp.maximum(scores[0].max(-1), scores[1].max(-1)), scores[2].max(-1))
    total = 0.0
    weighted = 0.0
    for step in range(3):
        weight = jnp.exp(scores[step] - top[..., None])
        total = total + weight.sum(-1)
        weighted = weighted + jnp.einsum(
            "shqk,skhd->sqhd", weight.astype(BF16), values[step], preferred_element_type=F32
        )
    attended = weighted / jnp.transpose(total, (0, 2, 1))[..., None]
    return attended, top + jnp.log(total)


def attend_backward(query, keys, values, grad_heads, attended, log_total, context):
    scale = HD ** (-0.5)
    delta = jnp.transpose(jnp.sum(grad_heads.astype(F32) * attended, axis=3), (0, 2, 1))
    grad_query = 0.0
    grad_keys, grad_values = [], []
    for step in range(3):
        raw = jnp.einsum("sqhd,skhd->shqk", query, keys[step], preferred_element_type=F32) * scale
        weight = jnp.where(
            allowed_mask(context, step)[:, None], jnp.exp(raw - log_total[..., None]), 0.0
        )
        grad_weight = jnp.einsum(
            "sqhd,skhd->shqk", grad_heads, values[step], preferred_element_type=F32
        )
        grad_scores = (weight * (grad_weight - delta[..., None])).astype(BF16)
        grad_query = grad_query + jnp.einsum(
            "shqk,skhd->sqhd", grad_scores, keys[step], preferred_element_type=F32
        )
        grad_keys.append(
            jnp.einsum("shqk,sqhd->skhd", grad_scores, query, preferred_element_type=F32) * scale
        )
        grad_values.append(
            jnp.einsum(
                "shqk,sqhd->skhd", weight.astype(BF16), grad_heads, preferred_element_type=F32
            )
        )
    return grad_query * scale, grad_keys, grad_values


def own_half(values, axis, size, pair):
    start = pair * (values.shape[axis] - size)
    return lax.dynamic_slice_in_dim(values, start, size, axis)


def whole_weights(layer, pair):
    w_qkv, b_qkv, w_out, w_gate_up, w_down = layer
    units = w_down.shape[0]
    columns = w_out.shape[0] // 2
    unit_count = -(-(units // 2) // LANES) * LANES
    down_part = own_half(w_down, 0, unit_count, pair)
    shared = 2 * unit_count - units
    if shared:
        repeated = (jnp.arange(unit_count) < shared)[:, None] & (pair == 1)
        down_part = jnp.where(repeated, jnp.zeros_like(down_part), down_part)
    return (
        lax.all_gather(own_half(w_qkv, 2, columns, pair), "fsdp", axis=1, tiled=True),
        own_half(lax.all_gather(b_qkv, "fsdp", axis=2, tiled=True), 1, b_qkv.shape[1] // 2, pair),
        lax.all_gather(own_half(w_out, 0, columns, pair), "fsdp", axis=1, tiled=True),
        lax.all_gather(own_half(w_gate_up, 2, unit_count, pair), "fsdp", axis=1, tiled=True),
        lax.all_gather(down_part, "fsdp", axis=1, tiled=True),
    )


def forward_layer(stream, weights, gain_rows, shift_rows, context):
    w_qkv, b_qkv, w_out, w_gate_up, w_down = weights
    attention_context, cosine, sine_table = context
    heads = b_qkv.shape[1]
    normed, scaled_one, recip_one = norm_forward(stream, gain_rows[0], shift_rows[0])
    first_in = gather_rows(normed.astype(BF16))
    rows = first_in.shape[0]
    mixed = jnp.einsum("td,cde->cte", first_in, w_qkv, preferred_element_type=F32)
    mixed = mixed + b_qkv.astype(F32).reshape(3, 1, heads * HD)
    mixed = mixed.reshape(3, rows, heads, HD)
    query = rotate(mixed[0], cosine, sine_table).astype(BF16).reshape(rows, heads * HD)
    key = rotate(mixed[1], cosine, sine_table).astype(BF16).reshape(rows, heads * HD)
    value = mixed[2].astype(BF16).reshape(rows, heads * HD)
    blocks = key_blocks(jnp.concatenate([key, value], 1), heads)
    query = by_sequence(query, heads)
    keys = [by_sequence(blocks[i][:, : heads * HD], heads) for i in range(3)]
    values = [by_sequence(blocks[i][:, heads * HD :], heads) for i in range(3)]
    attended, log_total = attend(query, keys, values, attention_context)
    att_low = by_row(attended.astype(BF16))
    stream_h = stream + scatter_rows(
        jnp.dot(att_low, w_out, preferred_element_type=F32).astype(BF16)
    )
    normed_two, scaled_two, recip_two = norm_forward(stream_h, gain_rows[1], shift_rows[1])
    second_in = gather_rows(normed_two.astype(BF16))
    gate_up = jnp.einsum("td,cdf->ctf", second_in, w_gate_up, preferred_element_type=F32)
    activated = (jax.nn.silu(gate_up[0]) * gate_up[1]).astype(BF16)
    result = stream_h + scatter_rows(
        jnp.dot(activated, w_down, preferred_element_type=F32).astype(BF16)
    )
    stored = (
        scaled_one,
        recip_one,
        first_in,
        query,
        keys,
        values,
        attended,
        log_total,
        att_low,
        scaled_two,
        recip_two,
        second_in,
        gate_up,
        activated,
    )
    return (result, stored)


def scatter_weight(gradient, axis):
    return lax.psum_scatter(gradient.astype(BF16), "fsdp", scatter_dimension=axis, tiled=True)


def other_pairs(shard):
    count = lax.axis_size("replica")
    pair = pair_size()
    total = shard.astype(F32)
    for step in range(pair, count, pair):
        total = total + lax.ppermute(
            shard, "replica", [(i, (i + step) % count) for i in range(count)]
        ).astype(F32)
    return total.astype(BF16)


def join_halves(shard, axis, size, pair):
    mine = other_pairs(shard)
    theirs = swap_replica(mine)
    extra = 2 * shard.shape[axis] - size
    first = jnp.where(pair == 0, mine, theirs).astype(F32)
    second = jnp.where(pair == 0, theirs, mine).astype(F32)
    second = lax.slice_in_dim(second, extra, second.shape[axis], axis=axis)
    return jnp.concatenate([first, second], axis)


def backward_layer(grad_stream, weights, gain_rows, stored, context, pair, sizes):
    w_qkv, b_qkv, w_out, w_gate_up, w_down = weights
    attention_context, cosine, sine_table = context
    (
        scaled_one,
        recip_one,
        first_in,
        query,
        keys,
        values,
        attended,
        log_total,
        att_low,
        scaled_two,
        recip_two,
        second_in,
        gate_up,
        activated,
    ) = stored
    columns, units = sizes
    heads = b_qkv.shape[1]
    grad_out = gather_rows(grad_stream.astype(BF16))
    rows = grad_out.shape[0]
    grad_act = jnp.einsum("td,fd->tf", grad_out, w_down, preferred_element_type=F32)
    gate_part, up_part = gate_up[0], gate_up[1]
    sigmoid_gate = jax.nn.sigmoid(gate_part)
    grad_gate = grad_act * up_part * sigmoid_gate * (1.0 + gate_part * (1.0 - sigmoid_gate))
    grad_up = grad_act * gate_part * sigmoid_gate
    grad_mix_two = jnp.stack([grad_gate, grad_up]).astype(BF16)
    back = jnp.einsum("ctf,cdf->td", grad_mix_two, w_gate_up, preferred_element_type=F32)
    grad_norm_two = scatter_rows(back.astype(BF16))
    grad_down = scatter_weight(
        jnp.einsum("tf,td->fd", activated, grad_out, preferred_element_type=F32), 1
    )
    grad_gate_up = scatter_weight(
        jnp.einsum("td,ctf->cdf", second_in, grad_mix_two, preferred_element_type=F32), 1
    )
    back_two, gain_grad_two, shift_grad_two = norm_backward(
        grad_norm_two, scaled_two, recip_two, gain_rows[1]
    )
    grad_hidden = grad_stream + back_two
    grad_att = gather_rows(grad_hidden.astype(BF16))
    grad_heads = jnp.einsum("td,ed->te", grad_att, w_out, preferred_element_type=F32)
    grad_heads = by_sequence(grad_heads.astype(BF16), heads)
    grad_wout = scatter_weight(
        jnp.einsum("te,td->ed", att_low, grad_att, preferred_element_type=F32), 1
    )
    grad_query, grad_keys, grad_values = attend_backward(
        query, keys, values, grad_heads, attended, log_total, attention_context
    )
    packed = [
        jnp.concatenate([by_row(k), by_row(v)], 1) for k, v in zip(grad_keys, grad_values)
    ]
    returned = shift_fsdp(packed[2].astype(BF16), -1)
    returned = shift_fsdp((packed[1] + returned.astype(F32)).astype(BF16), -1)
    own = (packed[0] + returned.astype(F32)).astype(BF16)
    grad_query = by_row(grad_query.astype(BF16)).reshape(rows, heads, HD).astype(F32)
    grad_key = own[:, : heads * HD].reshape(rows, heads, HD).astype(F32)
    grad_value = own[:, heads * HD :]
    grad_mixed = jnp.stack(
        [
            rotate(grad_query, cosine, -sine_table).astype(BF16).reshape(rows, heads * HD),
            rotate(grad_key, cosine, -sine_table).astype(BF16).reshape(rows, heads * HD),
            grad_value,
        ]
    )
    back = jnp.einsum("cte,cde->td", grad_mixed, w_qkv, preferred_element_type=F32)
    grad_norm_one = scatter_rows(back.astype(BF16))
    grad_wqkv = scatter_weight(
        jnp.einsum("td,cte->cde", first_in, grad_mixed, preferred_element_type=F32), 1
    )
    grad_bias = jnp.sum(grad_mixed, axis=1, dtype=F32)
    back_one, gain_grad_one, shift_grad_one = norm_backward(
        grad_norm_one, scaled_one, recip_one, gain_rows[0]
    )
    grad_input = grad_hidden + back_one
    joined = (
        join_halves(grad_wqkv, 2, columns, pair),
        join_halves(grad_wout, 0, columns, pair),
        join_halves(grad_gate_up, 2, units, pair),
        join_halves(grad_down, 0, units, pair),
    )
    norm_grads = jnp.stack([gain_grad_one, gain_grad_two, shift_grad_one, shift_grad_two])
    return (grad_input, joined, norm_grads, grad_bias)


def body(tokens, segments, w_qkv, b_qkv, w_out, w_gate_up, w_down, ln_gain, ln_bias, cotangent):
    layers = w_qkv.shape[0]
    row_count = tokens.shape[1]
    tensor_count = lax.axis_size("tensor")
    group_rows = row_count * tensor_count
    replica = lax.axis_index("replica")
    pair = replica % 2
    block = lax.axis_index("fsdp")
    own = lax.axis_index("tensor")

    norms = lax.all_gather(
        jnp.stack([ln_gain, ln_bias]), ("fsdp", "tensor"), axis=3, tiled=True
    ).astype(F32)
    gain_all, shift_all = norms[0], norms[1]

    both_segments = jnp.concatenate([segments, swap_replica(segments)], 0)
    starts = lax.dynamic_slice_in_dim(
        segment_starts(both_segments), block * group_rows, group_rows, 1
    )
    index = block * group_rows + jnp.arange(group_rows, dtype=jnp.int32)
    index = jnp.broadcast_to(index[None, :], starts.shape)
    shape = (2, tensor_count, 2, row_count // 2)
    row_start = order_rows(starts.reshape(shape), own)
    row_index = order_rows(index.reshape(shape), own)
    cosine, sine_table = rotary_tables(row_index - row_start)

    def split(flat):
        return jnp.transpose(flat.reshape(4, 2, -1), (1, 0, 2)).reshape(2, -1)

    attention_context = (split(row_index), split(row_start), group_rows)
    context = (attention_context, cosine, sine_table)

    stream = tokens[0].astype(F32)
    kept = []
    for layer in range(layers):
        weights = whole_weights(
            (w_qkv[layer], b_qkv[layer], w_out[layer], w_gate_up[layer], w_down[layer]), pair
        )
        stream, stored = forward_layer(stream, weights, gain_all[layer], shift_all[layer], context)
        kept.append((weights, stored))
    output = stream.astype(BF16)[None]

    grad_stream = cotangent[0].astype(F32)
    joined = [None] * layers
    norm_parts = [None] * layers
    bias_parts = [None] * layers
    sizes = (w_qkv.shape[3], w_down.shape[1])
    for layer in reversed(range(layers)):
        weights, stored = kept[layer]
        grad_stream, joined[layer], norm_parts[layer], bias_parts[layer] = backward_layer(
            grad_stream, weights, gain_all[layer], stored, context, pair, sizes
        )

    norm_flat = jnp.stack(norm_parts).reshape(-1)
    bias_flat = jnp.stack(bias_parts)
    groups = 2 * tensor_count
    bias_count = bias_flat.size
    slots = jnp.zeros((groups, bias_count), F32)
    slots = lax.dynamic_update_slice(
        slots, bias_flat.reshape(1, bias_count), (own * 2 + pair, jnp.int32(0))
    )
    summed = lax.psum(
        jnp.concatenate([norm_flat, slots.reshape(-1)]), ("replica", "fsdp", "tensor")
    )
    width = stream.shape[1]
    norm_sum = summed[: norm_flat.size].reshape(layers, 4, width)
    slice_width = ln_gain.shape[2]
    norm_sum = lax.dynamic_slice_in_dim(
        norm_sum, (block * tensor_count + own) * slice_width, slice_width, 2
    )
    grad_gain, grad_shift = norm_sum[:, :2], norm_sum[:, 2:]
    bias_sum = summed[norm_flat.size :].reshape(groups, layers, 3, -1, HD)
    bias_sum = lax.dynamic_slice_in_dim(bias_sum, own * 2, 2, 0)
    bias_sum = jnp.transpose(bias_sum, (1, 2, 0, 3, 4)).reshape(layers, 3, b_qkv.shape[2], HD)
    bias_width = b_qkv.shape[3]
    grad_bias = lax.dynamic_slice_in_dim(bias_sum, block * bias_width, bias_width, 3)

    stacked = [jnp.stack([joined[layer][i] for layer in range(layers)]) for i in range(4)]
    return (
        output,
        grad_stream[None],
        stacked[0],
        grad_bias,
        stacked[1],
        stacked[2],
        stacked[3],
        grad_gain,
        grad_shift,
    )


def solution(mesh):
    return jax.shard_map(
        body,
        mesh=mesh,
        in_specs=(
            P("replica", ("fsdp", "tensor"), None),
            P("replica", None),
            P(None, None, "fsdp", "tensor"),
            P(None, None, "tensor", "fsdp"),
            P(None, "tensor", "fsdp"),
            P(None, None, "fsdp", "tensor"),
            P(None, "tensor", "fsdp"),
            P(None, None, ("fsdp", "tensor")),
            P(None, None, ("fsdp", "tensor")),
            P("replica", ("fsdp", "tensor"), None),
        ),
        out_specs=(
            P("replica", ("fsdp", "tensor"), None),
            P("replica", ("fsdp", "tensor"), None),
            P(None, None, "fsdp", "tensor"),
            P(None, None, "tensor", "fsdp"),
            P(None, "tensor", "fsdp"),
            P(None, None, "fsdp", "tensor"),
            P(None, "tensor", "fsdp"),
            P(None, None, ("fsdp", "tensor")),
            P(None, None, ("fsdp", "tensor")),
        ),
        check_vma=False,
    )
```

```python
import jax
import jax.numpy as jnp
from jax import lax
from jax.experimental import pallas as pl
from jax.experimental.pallas import tpu as pltpu
from jax.sharding import PartitionSpec as P

HD = 64
ROT = 16
EPSILON = 1e-05
MASKED = -1e30
LANES = 128
F32 = jnp.float32
BF16 = jnp.bfloat16


def pair_size():
    return 2 if lax.axis_size("replica") % 2 == 0 else 1


def swap_tensor(values, bit):
    count = lax.axis_size("tensor")
    return lax.ppermute(values, "tensor", [(i, i ^ bit) for i in range(count)])


def swap_replica(values):
    count = lax.axis_size("replica")
    return lax.ppermute(values, "replica", [(i, i ^ 1) for i in range(count)])


def shift_fsdp(values, step):
    count = lax.axis_size("fsdp")
    return lax.ppermute(
        values, "fsdp", [(i, i + step) for i in range(count) if 0 <= i + step < count]
    )


def gather_rows(rows):
    half = rows.shape[0] // 2
    a_own, b_own = rows[:half], rows[half:]
    a_y = swap_tensor(a_own, 2)
    b_x = swap_replica(b_own)
    a_y, b_x = lax.optimization_barrier((a_y, b_x))
    a_pair = jnp.concatenate([a_own, a_y], 0)
    b_pair = jnp.concatenate([b_own, b_x], 0)
    a_x = swap_replica(a_pair)
    b_y = swap_tensor(b_pair, 2)
    a_x, b_y = lax.optimization_barrier((a_x, b_y))
    mine = jnp.concatenate([a_pair, a_x, b_own, b_y[:half], b_x, b_y[half:]], 0)
    other = swap_tensor(mine, 1)
    return jnp.concatenate([mine, other], 0)


def add_low(first, second):
    return (first.astype(F32) + second.astype(F32)).astype(BF16)


def scatter_rows(partial):
    total, width = partial.shape
    half = total // 16
    received = swap_tensor(partial[total // 2 :], 1)
    mine = add_low(partial[: total // 2], received).reshape(2, 2, 2, half, width)
    a_part, b_part = mine[0], mine[1]
    a_in = swap_replica(a_part[1])
    b_in = swap_tensor(b_part[:, 1], 2)
    a_part = add_low(a_part[0], a_in)
    b_part = add_low(b_part[:, 0], b_in)
    a_in = swap_tensor(a_part[1], 2)
    b_in = swap_replica(b_part[1])
    a_row = a_part[0].astype(F32) + a_in.astype(F32)
    b_row = b_part[0].astype(F32) + b_in.astype(F32)
    return jnp.concatenate([a_row, b_row], 0)


def order_rows(blocks, own):
    picked = [
        [lax.dynamic_index_in_dim(blocks, own ^ (2 * y + c), 1, keepdims=False) for y in range(2)]
        for c in range(2)
    ]
    stacked = jnp.stack([jnp.stack(row) for row in picked])
    return jnp.transpose(stacked, (0, 3, 2, 1, 4)).reshape(-1)


def segment_starts(segment_rows):
    length = segment_rows.shape[1]
    index = jnp.arange(length, dtype=jnp.int32)
    earlier = jnp.concatenate([segment_rows[:, :1] - 1, segment_rows[:, :-1]], 1)
    boundary = jnp.where(segment_rows != earlier, index[None, :], 0)
    return lax.cummax(boundary, axis=1)


def rotary_tables(positions):
    half_width = ROT // 2
    lane = jnp.arange(LANES, dtype=jnp.int32) % HD
    frequency = jnp.exp(-jnp.log(10000.0) * (lane % half_width).astype(F32) * 2.0 / ROT)
    frequency = jnp.where(lane < ROT, frequency, 0.0)
    sign = jnp.where(lane < half_width, -1.0, 1.0)
    angles = positions.astype(F32)[:, None] * frequency[None, :]
    return (jnp.cos(angles), jnp.sin(angles) * sign[None, :])


def rotated(values, cosine, sine):
    half_width = ROT // 2
    lane = lax.broadcasted_iota(jnp.int32, values.shape, 1) % HD
    swapped = jnp.where(
        lane < half_width,
        pltpu.roll(values, LANES - half_width, 1),
        pltpu.roll(values, half_width, 1),
    )
    return values * cosine + swapped * sine


def project_kernel(mixed_ref, bias_ref, cos_ref, sin_ref, query_ref, packed_ref):
    cosine, sine = cos_ref[...], sin_ref[...]
    for duo in range(query_ref.shape[1] // LANES):
        lanes = slice(duo * LANES, (duo + 1) * LANES)
        query = rotated(mixed_ref[0, :, lanes] + bias_ref[0, :, lanes], cosine, sine)
        query_ref[:, lanes] = (query.astype(BF16).astype(F32) * HD ** (-0.5)).astype(BF16)
        key = rotated(mixed_ref[1, :, lanes] + bias_ref[1, :, lanes], cosine, sine)
        value = mixed_ref[2, :, lanes] + bias_ref[2, :, lanes]
        start = 2 * duo * LANES
        packed_ref[:, start : start + LANES] = key.astype(BF16)
        packed_ref[:, start + LANES : start + 2 * LANES] = value.astype(BF16)


def project(mixed, bias, cosine, sine):
    _, rows, width = mixed.shape
    tile = min(256, rows)
    return pl.pallas_call(
        project_kernel,
        grid=(rows // tile,),
        in_specs=[
            pl.BlockSpec((3, tile, width), lambda i: (0, i, 0)),
            pl.BlockSpec((3, 1, width), lambda i: (0, 0, 0)),
            pl.BlockSpec((tile, LANES), lambda i: (i, 0)),
            pl.BlockSpec((tile, LANES), lambda i: (i, 0)),
        ],
        out_specs=[
            pl.BlockSpec((tile, width), lambda i: (i, 0)),
            pl.BlockSpec((tile, 2 * width), lambda i: (i, 0)),
        ],
        out_shape=[
            jax.ShapeDtypeStruct((rows, width), BF16),
            jax.ShapeDtypeStruct((rows, 2 * width), BF16),
        ],
        name="project",
    )(mixed, bias, cosine, sine)


def unproject_query_kernel(query_ref, cos_ref, sin_ref, mixed_ref):
    for duo in range(query_ref.shape[1] // LANES):
        lanes = slice(duo * LANES, (duo + 1) * LANES)
        mixed_ref[:, lanes] = rotated(
            query_ref[:, lanes].astype(F32), cos_ref[...], -sin_ref[...]
        ).astype(BF16)


def unproject_query(grad_query, cosine, sine):
    rows, width = grad_query.shape
    tile = min(256, rows)
    return pl.pallas_call(
        unproject_query_kernel,
        grid=(rows // tile,),
        in_specs=[
            pl.BlockSpec((tile, width), lambda i: (i, 0)),
            pl.BlockSpec((tile, LANES), lambda i: (i, 0)),
            pl.BlockSpec((tile, LANES), lambda i: (i, 0)),
        ],
        out_specs=pl.BlockSpec((tile, width), lambda i: (i, 0)),
        out_shape=jax.ShapeDtypeStruct((rows, width), BF16),
        name="unproject_query",
    )(grad_query, cosine, sine)


def unproject_kernel(own_ref, back_ref, cos_ref, sin_ref, mixed_ref):
    cosine, sine = cos_ref[...], -sin_ref[...]
    for duo in range(mixed_ref.shape[2] // LANES):
        lanes = slice(duo * LANES, (duo + 1) * LANES)
        start = 2 * duo * LANES
        here = slice(start, start + LANES)
        key = (own_ref[:, here] + back_ref[:, here].astype(F32)).astype(BF16).astype(F32)
        mixed_ref[0, :, lanes] = rotated(key, cosine, sine).astype(BF16)
        here = slice(start + LANES, start + 2 * LANES)
        mixed_ref[1, :, lanes] = (own_ref[:, here] + back_ref[:, here].astype(F32)).astype(BF16)


def unproject(own, back, cosine, sine):
    rows, width = own.shape[0], own.shape[1] // 2
    tile = min(256, rows)
    return pl.pallas_call(
        unproject_kernel,
        grid=(rows // tile,),
        in_specs=[
            pl.BlockSpec((tile, 2 * width), lambda i: (i, 0)),
            pl.BlockSpec((tile, 2 * width), lambda i: (i, 0)),
            pl.BlockSpec((tile, LANES), lambda i: (i, 0)),
            pl.BlockSpec((tile, LANES), lambda i: (i, 0)),
        ],
        out_specs=pl.BlockSpec((2, tile, width), lambda i: (0, i, 0)),
        out_shape=jax.ShapeDtypeStruct((2, rows, width), BF16),
        name="unproject",
    )(own, back, cosine, sine)


def norm_forward(stream, gain_row, shift_row):
    average = jnp.mean(stream, axis=-1, keepdims=True)
    centred = stream - average
    variance = jnp.mean(centred * centred, axis=-1, keepdims=True)
    reciprocal = lax.rsqrt(variance + EPSILON)
    scaled = centred * reciprocal
    return (scaled * gain_row + shift_row, scaled, reciprocal)


def norm_backward(gradient, scaled, reciprocal, gain_row):
    weighted_grad = gradient * gain_row
    result = reciprocal * (
        weighted_grad
        - jnp.mean(weighted_grad, axis=-1, keepdims=True)
        - scaled * jnp.mean(weighted_grad * scaled, axis=-1, keepdims=True)
    )
    return (result, jnp.sum(gradient * scaled, axis=0), jnp.sum(gradient, axis=0))


def mask_rows(bias_ref, key_ref, index_ref, start_ref, row_count):
    query_index, query_start = index_ref[0], start_ref[0]
    for step in range(3):

        def fill(chunk, carry, step=step):
            key_index = key_ref[0, pl.ds(chunk * LANES, LANES), :] - step * row_count
            allowed = (key_index <= query_index) & (key_index >= query_start)
            rows = pl.ds(step * row_count + chunk * LANES, LANES)
            bias_ref[rows, :] = jnp.where(allowed, 0.0, MASKED)
            return carry

        lax.fori_loop(0, row_count // LANES, fill, 0)


def one_head(values, which):
    lane = lax.broadcasted_iota(jnp.int32, values.shape, 1)
    return jnp.where(lane // HD == which, values, jnp.zeros_like(values))


def dot_lanes(first, second):
    return lax.dot_general(first, second, (((1,), (1,)), ((), ())), preferred_element_type=F32)


def dot_rows(first, second):
    return lax.dot_general(first, second, (((0,), (0,)), ((), ())), preferred_element_type=F32)


def fold(values, operation):
    return operation(values.reshape(values.shape[0] // 8, 8, values.shape[1]), axis=0)


def attend_kernel(
    index_ref, start_ref, key_ref, query_ref, own_ref, before_ref, earlier_ref,
    turned_ref, low_ref, log_ref, bias_ref, score_ref, weight_ref,
):
    row_count = index_ref.shape[2]
    chunks = row_count // LANES

    @pl.when(pl.program_id(1) == 0)
    def _():
        mask_rows(bias_ref, key_ref, index_ref, start_ref, row_count)

    query = query_ref[...].reshape(row_count, LANES)
    blocks = (own_ref, before_ref, earlier_ref)
    for which in range(2):
        picked = one_head(query, which)
        top = jnp.full((8, row_count), MASKED, F32)
        for step in range(3):

            def score(chunk, top, step=step):
                rows = pl.ds(step * row_count + chunk * LANES, LANES)
                raw = dot_lanes(blocks[step][chunk, 0, :, :LANES], picked) + bias_ref[rows, :]
                score_ref[rows, :] = raw
                return jnp.maximum(top, fold(raw, jnp.max))

            top = lax.fori_loop(0, chunks, score, top)
        top = jnp.max(top, axis=0, keepdims=True)

        def soften(chunk, total):
            rows = pl.ds(chunk * LANES, LANES)
            weight = jnp.exp(score_ref[rows, :] - top)
            weight_ref[rows, :] = weight.astype(BF16)
            return total + fold(weight, jnp.sum)

        total = lax.fori_loop(0, 3 * chunks, soften, jnp.zeros((8, row_count), F32))
        total = jnp.sum(total, axis=0, keepdims=True)
        weighted = jnp.zeros((LANES, row_count), F32)
        for step in range(3):
            value = blocks[step][:, 0, :, LANES:].reshape(row_count, LANES)
            weighted = weighted + dot_rows(
                value, weight_ref[step * row_count : (step + 1) * row_count, :]
            )
        here = slice(which * HD, (which + 1) * HD)
        turned_ref[0, 0, here, :] = weighted[here, :] / total
        log_ref[0, 0, which : which + 1, :] = top + jnp.log(total)
    low_ref[...] = jnp.transpose(turned_ref[0, 0]).astype(BF16).reshape(low_ref.shape)


def sequence_block(width):
    return pl.BlockSpec((4, 1, LANES, width), lambda s, p: (0, s, 0, p))


def index_specs(row_count):
    return [
        pl.BlockSpec((1, 1, row_count), lambda s, p: (s, 0, 0)),
        pl.BlockSpec((1, 1, row_count), lambda s, p: (s, 0, 0)),
        pl.BlockSpec((1, row_count, 1), lambda s, p: (s, 0, 0)),
    ]


def attend(query, blocks, context):
    rows, width = query.shape
    row_count, duos = rows // 2, width // LANES
    pair_spec = pl.BlockSpec((1, 1, LANES, row_count), lambda s, p: (s, p, 0, 0))
    log_spec = pl.BlockSpec((1, 1, 2, row_count), lambda s, p: (s, p, 0, 0))
    turned, low, log_total = pl.pallas_call(
        attend_kernel,
        grid=(2, duos),
        in_specs=index_specs(row_count) + [sequence_block(LANES)] + [sequence_block(2 * LANES)] * 3,
        out_specs=[pair_spec, sequence_block(LANES), log_spec],
        out_shape=[
            jax.ShapeDtypeStruct((2, duos, LANES, row_count), F32),
            jax.ShapeDtypeStruct((4, 2, LANES, width), BF16),
            jax.ShapeDtypeStruct((2, duos, 2, row_count), F32),
        ],
        scratch_shapes=[
            pltpu.VMEM((3 * row_count, row_count), F32),
            pltpu.VMEM((3 * row_count, row_count), F32),
            pltpu.VMEM((3 * row_count, row_count), BF16),
        ],
        name="attend",
    )(*context, query.reshape(4, 2, LANES, width), *blocks)
    return turned, low.reshape(rows, width), log_total


def attend_back_kernel(
    index_ref, start_ref, key_ref, query_ref, own_ref, before_ref, earlier_ref,
    grad_ref, turned_ref, log_ref,
    query_out, own_out, before_out, earlier_out, bias_ref, score_ref,
):
    row_count = index_ref.shape[2]
    chunks = row_count // LANES

    @pl.when(pl.program_id(1) == 0)
    def _():
        mask_rows(bias_ref, key_ref, index_ref, start_ref, row_count)

    query = query_ref[...].reshape(row_count, LANES)
    grad = grad_ref[...].reshape(row_count, LANES)
    product = jnp.transpose(grad.astype(F32)) * turned_ref[0, 0]
    delta = [
        jnp.sum(product[which * HD : (which + 1) * HD], axis=0, keepdims=True)
        for which in range(2)
    ]
    queries = [one_head(query, which) for which in range(2)]
    grads = [one_head(grad, which) for which in range(2)]
    blocks = (own_ref, before_ref, earlier_ref)
    outs = (own_out, before_out, earlier_out)
    for step in range(3):

        def back(chunk, carry, step=step):
            rows = pl.ds(step * row_count + chunk * LANES, LANES)
            key = blocks[step][chunk, 0, :, :LANES]
            value = blocks[step][chunk, 0, :, LANES:]
            grad_key = jnp.zeros((LANES, LANES), F32)
            grad_value = jnp.zeros((LANES, LANES), F32)
            for which in range(2):
                raw = dot_lanes(key, queries[which]) + bias_ref[rows, :]
                weight = jnp.exp(raw - log_ref[0, 0, which : which + 1, :])
                grad_weight = dot_lanes(value, grads[which])
                grad_score = (weight * (grad_weight - delta[which])).astype(BF16)
                score_ref[which, rows, :] = grad_score
                grad_key = grad_key + jnp.dot(
                    grad_score, queries[which], preferred_element_type=F32
                )
                grad_value = grad_value + jnp.dot(
                    weight.astype(BF16), grads[which], preferred_element_type=F32
                )
            outs[step][chunk, 0, :, :LANES] = grad_key.astype(outs[step].dtype)
            outs[step][chunk, 0, :, LANES:] = grad_value.astype(outs[step].dtype)
            return carry

        lax.fori_loop(0, chunks, back, 0)
    parts = []
    for which in range(2):
        turned = jnp.zeros((LANES, row_count), F32)
        for step in range(3):
            key = blocks[step][:, 0, :, :LANES].reshape(row_count, LANES)
            turned = turned + dot_rows(
                key, score_ref[which, step * row_count : (step + 1) * row_count, :]
            )
        parts.append(turned[which * HD : (which + 1) * HD])
    turned = jnp.concatenate(parts, 0) * HD ** (-0.5)
    query_out[...] = jnp.transpose(turned).astype(BF16).reshape(query_out.shape)


def attend_backward(query, blocks, grad_heads, turned, log_total, context):
    rows, width = query.shape
    row_count, duos = rows // 2, width // LANES
    pair_spec = pl.BlockSpec((1, 1, LANES, row_count), lambda s, p: (s, p, 0, 0))
    log_spec = pl.BlockSpec((1, 1, 2, row_count), lambda s, p: (s, p, 0, 0))
    wide = (4, 2, LANES, 2 * width)
    grad_query, own, before, earlier = pl.pallas_call(
        attend_back_kernel,
        grid=(2, duos),
        in_specs=index_specs(row_count)
        + [sequence_block(LANES)]
        + [sequence_block(2 * LANES)] * 3
        + [sequence_block(LANES), pair_spec, log_spec],
        out_specs=[sequence_block(LANES)] + [sequence_block(2 * LANES)] * 3,
        out_shape=[
            jax.ShapeDtypeStruct((4, 2, LANES, width), BF16),
            jax.ShapeDtypeStruct(wide, F32),
            jax.ShapeDtypeStruct(wide, F32),
            jax.ShapeDtypeStruct(wide, BF16),
        ],
        scratch_shapes=[
            pltpu.VMEM((3 * row_count, row_count), F32),
            pltpu.VMEM((2, 3 * row_count, row_count), BF16),
        ],
        name="attend_back",
    )(
        *context, query.reshape(4, 2, LANES, width), *blocks,
        grad_heads.reshape(4, 2, LANES, width), turned, log_total,
    )
    flat = (rows, 2 * width)
    return (
        grad_query.reshape(rows, width),
        own.reshape(flat),
        before.reshape(flat),
        earlier.reshape(flat),
    )


def own_half(values, axis, size, pair):
    start = pair * (values.shape[axis] - size)
    return lax.dynamic_slice_in_dim(values, start, size, axis)


def weight_parts(layer, pair):
    w_qkv, b_qkv, w_out, w_gate_up, w_down = layer
    units = w_down.shape[0]
    columns = w_out.shape[0] // 2
    unit_count = -(-(units // 2) // LANES) * LANES
    down_part = own_half(w_down, 0, unit_count, pair)
    shared = 2 * unit_count - units
    if shared:
        repeated = (jnp.arange(unit_count) < shared)[:, None] & (pair == 1)
        down_part = jnp.where(repeated, jnp.zeros_like(down_part), down_part)
    return [
        own_half(w_qkv, 2, columns, pair),
        b_qkv,
        jnp.concatenate([own_half(w_out, 0, columns, pair), down_part], 0),
        own_half(w_gate_up, 2, unit_count, pair),
    ]


def whole(part):
    return lax.all_gather(part, "fsdp", axis=1, tiled=True)


def after(value, *others):
    return lax.optimization_barrier((value, *others))


def forward_layer(stream, parts, later, gain_rows, shift_rows, context):
    w_qkv, b_qkv, w_rows, w_gate_up = parts
    w_qkv, w_rows = whole(w_qkv), whole(w_rows)
    w_out, w_down = w_rows[: w_qkv.shape[2]], w_rows[w_qkv.shape[2] :]
    attention_context, cosine, sine_table = context
    heads = b_qkv.shape[1]
    normed, scaled_one, recip_one = norm_forward(stream, gain_rows[0], shift_rows[0])
    first_in = gather_rows(normed.astype(BF16))
    rows = first_in.shape[0]
    mixed = jnp.einsum("td,cde->cte", first_in, w_qkv, preferred_element_type=F32)
    bias = b_qkv.astype(F32).reshape(3, 1, heads * HD)
    query, packed = project(mixed, bias, cosine, sine_table)
    before = shift_fsdp(packed, 1)
    earlier = shift_fsdp(before, 1)
    earlier, w_gate_up, *later = after(earlier, w_gate_up, *later)
    w_gate_up = whole(w_gate_up)
    blocks = [part.reshape(4, 2, rows // 8, 2 * heads * HD) for part in (packed, before, earlier)]
    turned, att_low, log_total = attend(query, blocks, attention_context)
    stream_h = stream + scatter_rows(
        jnp.dot(att_low, w_out, preferred_element_type=F32).astype(BF16)
    )
    normed_two, scaled_two, recip_two = norm_forward(stream_h, gain_rows[1], shift_rows[1])
    second_in = gather_rows(normed_two.astype(BF16))
    gate_up = jnp.einsum("td,cdf->ctf", second_in, w_gate_up, preferred_element_type=F32)
    activated = (jax.nn.silu(gate_up[0]) * gate_up[1]).astype(BF16)
    result = stream_h + scatter_rows(
        jnp.dot(activated, w_down, preferred_element_type=F32).astype(BF16)
    )
    stored = (
        scaled_one,
        recip_one,
        first_in,
        query,
        blocks,
        turned,
        log_total,
        att_low,
        scaled_two,
        recip_two,
        second_in,
        gate_up,
        activated,
    )
    return (result, (w_qkv, b_qkv, w_out, w_gate_up, w_down), stored, later)


def scatter_weight(gradient, axis):
    return lax.psum_scatter(gradient.astype(BF16), "fsdp", scatter_dimension=axis, tiled=True)


def other_pairs(shard):
    count = lax.axis_size("replica")
    pair = pair_size()
    total = shard.astype(F32)
    for step in range(pair, count, pair):
        total = total + lax.ppermute(
            shard, "replica", [(i, (i + step) % count) for i in range(count)]
        ).astype(F32)
    return total.astype(BF16)


def sum_over(values, axis):
    count = lax.axis_size(axis)
    bit = 1
    while bit < count:
        values = values + lax.ppermute(values, axis, [(i, i ^ bit) for i in range(count)])
        bit *= 2
    return values


def place_lanes_kernel(pair_ref, mine_ref, theirs_ref, *rest):
    out_ref = rest[-1]
    size = mine_ref.shape[-1]
    extra = 2 * size - out_ref.shape[-1]

    def write(first, second):
        out_ref[0, 0, :, :size] = first[0].astype(F32)
        out_ref[0, 0, :, size:] = second[0, :, extra:].astype(F32)

    @pl.when(pair_ref[0] == 0)
    def _():
        write(mine_ref, theirs_ref)

    @pl.when(pair_ref[0] != 0)
    def _():
        write(theirs_ref, mine_ref)


def place_rows_kernel(pair_ref, mine_ref, theirs_ref, *rest):
    out_ref = rest[-1]
    size = mine_ref.shape[0]
    extra = 2 * size - out_ref.shape[1]

    def write(first, second):
        out_ref[0, :size] = first[...].astype(F32)
        out_ref[0, size:] = second[extra:].astype(F32)

    @pl.when(pair_ref[0] == 0)
    def _():
        write(mine_ref, theirs_ref)

    @pl.when(pair_ref[0] != 0)
    def _():
        write(theirs_ref, mine_ref)


def place_turned_kernel(pair_ref, mine_ref, theirs_ref, *rest):
    out_ref = rest[-1]
    size = mine_ref.shape[0]

    def write(first, second):
        out_ref[0, 0, :, :size] = jnp.transpose(first[...].astype(F32))
        out_ref[0, 0, :, size:] = jnp.transpose(second[...].astype(F32))

    @pl.when(pair_ref[0] == 0)
    def _():
        write(mine_ref, theirs_ref)

    @pl.when(pair_ref[0] != 0)
    def _():
        write(theirs_ref, mine_ref)


def exchange(shard):
    mine = other_pairs(shard)
    return mine, swap_replica(mine)


def place(both, layer, layers, buffer, pair, first=0, parts=None, units=None, turned=False):
    mine, theirs = both
    pair = pair.astype(jnp.int32).reshape(1)
    if parts is None:
        total = units
        size, width = min(mine.shape[0], -(-(total // 2) // LANES) * LANES), mine.shape[1]
        tile = LANES
        grid = (width // tile,)
        in_spec = pl.BlockSpec((size, tile), lambda i, p: (0, i))
        out_spec = pl.BlockSpec((1, total, tile), lambda i, p: (layer, 0, i))
        shape = (layers, total, width)
        kernel = place_rows_kernel
    elif turned:
        size, width = mine.shape[0] // 2, mine.shape[1]
        tile = min(256, width)
        grid = (width // tile,)
        in_spec = pl.BlockSpec((size, tile), lambda i, p: (1, i))
        out_spec = pl.BlockSpec((1, 1, tile, units), lambda i, p: (layer, first, i, 0))
        shape = (layers, parts, width, units)
        kernel = place_turned_kernel
    else:
        count, rows, size = mine.shape
        tile = min(256, rows)
        grid = (count, rows // tile)
        in_spec = pl.BlockSpec((1, tile, size), lambda c, i, p: (c, i, 0))
        out_spec = pl.BlockSpec((1, 1, tile, units), lambda c, i, p: (layer, c + first, i, 0))
        shape = (layers, parts, rows, units)
        kernel = place_lanes_kernel
    operands = [pair, mine, theirs]
    in_specs = [in_spec, in_spec]
    aliases = {}
    if buffer is not None:
        operands.append(buffer)
        in_specs.append(pl.BlockSpec(memory_space=pl.ANY))
        aliases = {3: 0}
    return pl.pallas_call(
        kernel,
        grid_spec=pltpu.PrefetchScalarGridSpec(
            num_scalar_prefetch=1, grid=grid, in_specs=in_specs, out_specs=out_spec
        ),
        out_shape=jax.ShapeDtypeStruct(shape, F32),
        input_output_aliases=aliases,
        name="place",
    )(*operands)


def backward_layer(grad_stream, weights, gain_rows, stored, context, pending):
    w_qkv, b_qkv, w_out, w_gate_up, w_down = weights
    attention_context, cosine, sine_table = context
    (
        scaled_one,
        recip_one,
        first_in,
        query,
        blocks,
        turned,
        log_total,
        att_low,
        scaled_two,
        recip_two,
        second_in,
        gate_up,
        activated,
    ) = stored
    heads = b_qkv.shape[1]
    grad_out = gather_rows(grad_stream.astype(BF16))
    rows = grad_out.shape[0]
    grad_act = jnp.einsum("td,fd->tf", grad_out, w_down, preferred_element_type=F32)
    gate_part, up_part = gate_up[0], gate_up[1]
    sigmoid_gate = jax.nn.sigmoid(gate_part)
    grad_gate = grad_act * up_part * sigmoid_gate * (1.0 + gate_part * (1.0 - sigmoid_gate))
    grad_up = grad_act * gate_part * sigmoid_gate
    grad_mix_two = jnp.stack([grad_gate, grad_up]).astype(BF16)
    back = jnp.einsum("ctf,cdf->td", grad_mix_two, w_gate_up, preferred_element_type=F32)
    grad_norm_two = scatter_rows(back.astype(BF16))
    if pending:
        grad_norm_two = after(grad_norm_two, *pending)[0]
    grad_down = exchange(
        scatter_weight(
            jnp.einsum("tf,td->fd", activated, grad_out, preferred_element_type=F32), 1
        )
    )
    grad_gate_up = exchange(
        scatter_weight(
            jnp.einsum("td,ctf->cdf", second_in, grad_mix_two, preferred_element_type=F32), 1
        )
    )
    back_two, gain_grad_two, shift_grad_two = norm_backward(
        grad_norm_two, scaled_two, recip_two, gain_rows[1]
    )
    grad_hidden = grad_stream + back_two
    grad_att = gather_rows(grad_hidden.astype(BF16))
    grad_heads = jnp.einsum("td,ed->te", grad_att, w_out, preferred_element_type=F32)
    grad_heads = grad_heads.astype(BF16)
    grad_wout = jnp.einsum("te,td->ed", att_low, grad_att, preferred_element_type=F32)
    grad_query, own, before, earlier = attend_backward(
        query, blocks, grad_heads, turned, log_total, attention_context
    )
    query_mixed = unproject_query(grad_query, cosine, sine_table)
    grad_wquery = jnp.einsum("te,td->ed", query_mixed, first_in, preferred_element_type=F32)
    grad_rows = jnp.concatenate([grad_wout.astype(BF16), grad_wquery.astype(BF16)], 0)
    earlier, before, grad_rows = after(
        earlier, before, grad_rows, grad_down[1], grad_gate_up[0]
    )[:3]
    grad_rows = exchange(scatter_weight(grad_rows, 1))
    returned = shift_fsdp(earlier, -1)
    returned = shift_fsdp((before + returned.astype(F32)).astype(BF16), -1)
    grad_mixed = unproject(own, returned, cosine, sine_table)
    back = jnp.einsum("te,de->td", query_mixed, w_qkv[0], preferred_element_type=F32)
    back = back + jnp.einsum("cte,cde->td", grad_mixed, w_qkv[1:], preferred_element_type=F32)
    grad_wkv = jnp.einsum("td,cte->cde", first_in, grad_mixed, preferred_element_type=F32)
    back, grad_wkv = after(back.astype(BF16), grad_wkv.astype(BF16))
    grad_wkv = exchange(scatter_weight(grad_wkv, 1))
    grad_norm_one = scatter_rows(back)
    if pending:
        grad_norm_one = after(grad_norm_one, grad_gate_up[1])[0]
    grad_bias = jnp.concatenate(
        [
            jnp.sum(query_mixed, axis=0, dtype=F32, keepdims=True),
            jnp.sum(grad_mixed, axis=1, dtype=F32),
        ],
        0,
    )
    back_one, gain_grad_one, shift_grad_one = norm_backward(
        grad_norm_one, scaled_one, recip_one, gain_rows[0]
    )
    grad_input = grad_hidden + back_one
    norm_grads = jnp.stack([gain_grad_one, gain_grad_two, shift_grad_one, shift_grad_two])
    return (
        grad_input,
        (grad_gate_up, grad_down, grad_rows, grad_wkv),
        norm_grads,
        grad_bias,
    )


def body(tokens, segments, w_qkv, b_qkv, w_out, w_gate_up, w_down, ln_gain, ln_bias, cotangent):
    layers = w_qkv.shape[0]
    row_count = tokens.shape[1]
    tensor_count = lax.axis_size("tensor")
    group_rows = row_count * tensor_count
    replica = lax.axis_index("replica")
    pair = replica % 2
    block = lax.axis_index("fsdp")
    own = lax.axis_index("tensor")

    small = jnp.concatenate([ln_gain.reshape(-1), ln_bias.reshape(-1), b_qkv.reshape(-1)])
    small = lax.all_gather(small.reshape(-1, LANES), ("fsdp", "tensor"), axis=0)
    blocks = lax.axis_size("fsdp")
    norm_size, shift_size = ln_gain.size, 2 * ln_gain.size
    small = small.reshape(blocks, tensor_count, -1)

    def whole_rows(flat):
        flat = flat.reshape(blocks * tensor_count, layers, 2, ln_gain.shape[2])
        return jnp.transpose(flat, (1, 2, 0, 3)).reshape(layers, 2, -1).astype(F32)

    gain_all = whole_rows(small[:, :, :norm_size])
    shift_all = whole_rows(small[:, :, norm_size:shift_size])
    biases = lax.dynamic_index_in_dim(small[:, :, shift_size:], own, 1, keepdims=False)
    biases = biases.reshape(blocks, layers, 3, b_qkv.shape[2], b_qkv.shape[3])
    biases = jnp.transpose(biases, (1, 2, 3, 0, 4)).reshape(layers, 3, b_qkv.shape[2], -1)
    biases = own_half(biases, 2, b_qkv.shape[2] // 2, pair)

    both_segments = jnp.concatenate([segments, swap_replica(segments)], 0)
    starts = lax.dynamic_slice_in_dim(
        segment_starts(both_segments), block * group_rows, group_rows, 1
    )
    index = block * group_rows + jnp.arange(group_rows, dtype=jnp.int32)
    index = jnp.broadcast_to(index[None, :], starts.shape)
    shape = (2, tensor_count, 2, row_count // 2)
    row_start = order_rows(starts.reshape(shape), own)
    row_index = order_rows(index.reshape(shape), own)
    cosine, sine_table = rotary_tables(row_index - row_start)

    def split(flat):
        return jnp.transpose(flat.reshape(4, 2, -1), (1, 0, 2)).reshape(2, -1)

    query_index = split(row_index)
    attention_context = (
        query_index[:, None, :],
        split(row_start)[:, None, :],
        query_index[:, :, None],
    )
    context = (attention_context, cosine, sine_table)

    stream = tokens[0].astype(F32)
    kept = []
    parts = [
        weight_parts(
            (w_qkv[layer], biases[layer], w_out[layer], w_gate_up[layer], w_down[layer]), pair
        )
        for layer in range(layers)
    ]
    for layer in range(layers):
        later = [part for following in parts[layer + 1 :] for part in (following[0], *following[2:])]
        stream, weights, stored, later = forward_layer(
            stream, parts[layer], later, gain_all[layer], shift_all[layer], context
        )
        for i, following in enumerate(parts[layer + 1 :]):
            following[0], following[2:] = later[3 * i], later[3 * i + 1 : 3 * i + 3]
        kept.append((weights, stored))
    output = stream.astype(BF16)[None]

    grad_stream = cotangent[0].astype(F32)
    norm_parts = [None] * layers
    bias_parts = [None] * layers
    buffers = [None] * 4
    columns, units = w_qkv.shape[3], w_down.shape[1]

    shards = [None] * layers
    pending = ()
    for layer in reversed(range(layers)):
        weights, stored = kept[layer]
        grad_stream, shards[layer], norm_parts[layer], bias_parts[layer] = backward_layer(
            grad_stream, weights, gain_all[layer], stored, context, pending
        )
        pending = (shards[layer][0][1], shards[layer][2][1], shards[layer][3][1])
    for layer in reversed(range(layers)):
        wide, down, rows, late = shards[layer]
        buffers[2] = place(wide, layer, layers, buffers[2], pair, parts=2, units=units)
        buffers[3] = place(down, layer, layers, buffers[3], pair, units=units)
        buffers[1] = place(rows, layer, layers, buffers[1], pair, units=columns)
        buffers[0] = place(
            rows, layer, layers, buffers[0], pair, parts=3, units=columns, turned=True
        )
        buffers[0] = place(
            late, layer, layers, buffers[0], pair, first=1, parts=3, units=columns
        )

    norm_flat = jnp.stack(norm_parts).reshape(-1)
    bias_flat = jnp.stack(bias_parts).reshape(-1)
    norm_count = norm_flat.shape[0]
    summed = sum_over(jnp.concatenate([norm_flat, bias_flat]).reshape(-1, LANES), "fsdp")
    bias_mine = summed[norm_count // LANES :]
    for bit in range(1, (lax.axis_size("replica") - 1).bit_length()):
        bias_mine = bias_mine + lax.ppermute(
            bias_mine, "replica", [(i, i ^ (1 << bit)) for i in range(lax.axis_size("replica"))]
        )
    bias_other = swap_replica(bias_mine)
    summed = sum_over(summed[: norm_count // LANES], "tensor")
    width = stream.shape[1]
    norm_sum = sum_over(summed, "replica").reshape(layers, 4, width)
    slice_width = ln_gain.shape[2]
    norm_sum = lax.dynamic_slice_in_dim(
        norm_sum, (block * tensor_count + own) * slice_width, slice_width, 2
    )
    grad_gain, grad_shift = norm_sum[:, :2], norm_sum[:, 2:]
    shape = (layers, 3, b_qkv.shape[2] // 2, HD)
    bias_mine, bias_other = bias_mine.reshape(shape), bias_other.reshape(shape)
    bias_sum = jnp.concatenate(
        [
            jnp.where(pair == 0, bias_mine, bias_other),
            jnp.where(pair == 0, bias_other, bias_mine),
        ],
        2,
    )
    bias_width = b_qkv.shape[3]
    grad_bias = lax.dynamic_slice_in_dim(bias_sum, block * bias_width, bias_width, 3)

    return (
        output,
        grad_stream[None],
        buffers[0],
        grad_bias,
        buffers[1],
        buffers[2],
        buffers[3],
        grad_gain,
        grad_shift,
    )


def solution(mesh):
    return jax.shard_map(
        body,
        mesh=mesh,
        in_specs=(
            P("replica", ("fsdp", "tensor"), None),
            P("replica", None),
            P(None, None, "fsdp", "tensor"),
            P(None, None, "tensor", "fsdp"),
            P(None, "tensor", "fsdp"),
            P(None, None, "fsdp", "tensor"),
            P(None, "tensor", "fsdp"),
            P(None, None, ("fsdp", "tensor")),
            P(None, None, ("fsdp", "tensor")),
            P("replica", ("fsdp", "tensor"), None),
        ),
        out_specs=(
            P("replica", ("fsdp", "tensor"), None),
            P("replica", ("fsdp", "tensor"), None),
            P(None, None, "fsdp", "tensor"),
            P(None, None, "tensor", "fsdp"),
            P(None, "tensor", "fsdp"),
            P(None, None, "fsdp", "tensor"),
            P(None, "tensor", "fsdp"),
            P(None, None, ("fsdp", "tensor")),
            P(None, None, ("fsdp", "tensor")),
        ),
        check_vma=False,
    )
```

```python
import jax
import jax.numpy as jnp
from jax import lax
from jax.experimental import pallas as pl
from jax.experimental.pallas import tpu as pltpu
from jax.sharding import PartitionSpec as P

HD = 64
ROT = 16
EPSILON = 1e-05
MASKED = -1e30
LANES = 128
F32 = jnp.float32
BF16 = jnp.bfloat16


def pair_size():
    return 2 if lax.axis_size("replica") % 2 == 0 else 1


def swap_tensor(values, bit):
    count = lax.axis_size("tensor")
    return lax.ppermute(values, "tensor", [(i, i ^ bit) for i in range(count)])


def swap_replica(values):
    count = lax.axis_size("replica")
    return lax.ppermute(values, "replica", [(i, i ^ 1) for i in range(count)])


def shift_fsdp(values, step):
    count = lax.axis_size("fsdp")
    return lax.ppermute(
        values, "fsdp", [(i, i + step) for i in range(count) if 0 <= i + step < count]
    )


def gather_rows(rows):
    half = rows.shape[0] // 2
    a_own, b_own = rows[:half], rows[half:]
    a_y = swap_tensor(a_own, 2)
    b_x = swap_replica(b_own)
    a_y, b_x = lax.optimization_barrier((a_y, b_x))
    a_pair = jnp.concatenate([a_own, a_y], 0)
    b_pair = jnp.concatenate([b_own, b_x], 0)
    a_x = swap_replica(a_pair)
    b_y = swap_tensor(b_pair, 2)
    a_x, b_y = lax.optimization_barrier((a_x, b_y))
    mine = jnp.concatenate([a_pair, a_x, b_own, b_y[:half], b_x, b_y[half:]], 0)
    other = swap_tensor(mine, 1)
    return jnp.concatenate([mine, other], 0)


def add_low(first, second):
    return (first.astype(F32) + second.astype(F32)).astype(BF16)


def scatter_rows(partial):
    total, width = partial.shape
    half = total // 16
    received = swap_tensor(partial[total // 2 :], 1)
    mine = add_low(partial[: total // 2], received).reshape(2, 2, 2, half, width)
    a_part, b_part = mine[0], mine[1]
    a_in = swap_replica(a_part[1])
    b_in = swap_tensor(b_part[:, 1], 2)
    a_part = add_low(a_part[0], a_in)
    b_part = add_low(b_part[:, 0], b_in)
    a_in = swap_tensor(a_part[1], 2)
    b_in = swap_replica(b_part[1])
    a_row = a_part[0].astype(F32) + a_in.astype(F32)
    b_row = b_part[0].astype(F32) + b_in.astype(F32)
    return jnp.concatenate([a_row, b_row], 0)


def order_rows(blocks, own):
    picked = [
        [lax.dynamic_index_in_dim(blocks, own ^ (2 * y + c), 1, keepdims=False) for y in range(2)]
        for c in range(2)
    ]
    stacked = jnp.stack([jnp.stack(row) for row in picked])
    return jnp.transpose(stacked, (0, 3, 2, 1, 4)).reshape(-1)


def segment_starts(segment_rows):
    length = segment_rows.shape[1]
    index = jnp.arange(length, dtype=jnp.int32)
    earlier = jnp.concatenate([segment_rows[:, :1] - 1, segment_rows[:, :-1]], 1)
    boundary = jnp.where(segment_rows != earlier, index[None, :], 0)
    return lax.cummax(boundary, axis=1)


def rotary_tables(positions):
    half_width = ROT // 2
    lane = jnp.arange(LANES, dtype=jnp.int32) % HD
    frequency = jnp.exp(-jnp.log(10000.0) * (lane % half_width).astype(F32) * 2.0 / ROT)
    frequency = jnp.where(lane < ROT, frequency, 0.0)
    sign = jnp.where(lane < half_width, -1.0, 1.0)
    angles = positions.astype(F32)[:, None] * frequency[None, :]
    return (jnp.cos(angles), jnp.sin(angles) * sign[None, :])


def rotated(values, cosine, sine):
    half_width = ROT // 2
    lane = lax.broadcasted_iota(jnp.int32, values.shape, 1) % HD
    swapped = jnp.where(
        lane < half_width,
        pltpu.roll(values, LANES - half_width, 1),
        pltpu.roll(values, half_width, 1),
    )
    return values * cosine + swapped * sine


def project_kernel(mixed_ref, bias_ref, cos_ref, sin_ref, query_ref, packed_ref):
    cosine, sine = cos_ref[...], sin_ref[...]
    for duo in range(query_ref.shape[1] // LANES):
        lanes = slice(duo * LANES, (duo + 1) * LANES)
        query = rotated(mixed_ref[0, :, lanes] + bias_ref[0, :, lanes], cosine, sine)
        query_ref[:, lanes] = (query.astype(BF16).astype(F32) * HD ** (-0.5)).astype(BF16)
        key = rotated(mixed_ref[1, :, lanes] + bias_ref[1, :, lanes], cosine, sine)
        value = mixed_ref[2, :, lanes] + bias_ref[2, :, lanes]
        start = 2 * duo * LANES
        packed_ref[:, start : start + LANES] = key.astype(BF16)
        packed_ref[:, start + LANES : start + 2 * LANES] = value.astype(BF16)


def project(mixed, bias, cosine, sine):
    _, rows, width = mixed.shape
    tile = min(256, rows)
    return pl.pallas_call(
        project_kernel,
        grid=(rows // tile,),
        in_specs=[
            pl.BlockSpec((3, tile, width), lambda i: (0, i, 0)),
            pl.BlockSpec((3, 1, width), lambda i: (0, 0, 0)),
            pl.BlockSpec((tile, LANES), lambda i: (i, 0)),
            pl.BlockSpec((tile, LANES), lambda i: (i, 0)),
        ],
        out_specs=[
            pl.BlockSpec((tile, width), lambda i: (i, 0)),
            pl.BlockSpec((tile, 2 * width), lambda i: (i, 0)),
        ],
        out_shape=[
            jax.ShapeDtypeStruct((rows, width), BF16),
            jax.ShapeDtypeStruct((rows, 2 * width), BF16),
        ],
        name="project",
    )(mixed, bias, cosine, sine)


def unproject_query_kernel(query_ref, cos_ref, sin_ref, mixed_ref):
    for duo in range(query_ref.shape[1] // LANES):
        lanes = slice(duo * LANES, (duo + 1) * LANES)
        mixed_ref[:, lanes] = rotated(
            query_ref[:, lanes].astype(F32), cos_ref[...], -sin_ref[...]
        ).astype(BF16)


def unproject_query(grad_query, cosine, sine):
    rows, width = grad_query.shape
    tile = min(256, rows)
    return pl.pallas_call(
        unproject_query_kernel,
        grid=(rows // tile,),
        in_specs=[
            pl.BlockSpec((tile, width), lambda i: (i, 0)),
            pl.BlockSpec((tile, LANES), lambda i: (i, 0)),
            pl.BlockSpec((tile, LANES), lambda i: (i, 0)),
        ],
        out_specs=pl.BlockSpec((tile, width), lambda i: (i, 0)),
        out_shape=jax.ShapeDtypeStruct((rows, width), BF16),
        name="unproject_query",
    )(grad_query, cosine, sine)


def unproject_kernel(own_ref, back_ref, cos_ref, sin_ref, mixed_ref):
    cosine, sine = cos_ref[...], -sin_ref[...]
    for duo in range(mixed_ref.shape[2] // LANES):
        lanes = slice(duo * LANES, (duo + 1) * LANES)
        start = 2 * duo * LANES
        here = slice(start, start + LANES)
        key = (own_ref[:, here] + back_ref[:, here].astype(F32)).astype(BF16).astype(F32)
        mixed_ref[0, :, lanes] = rotated(key, cosine, sine).astype(BF16)
        here = slice(start + LANES, start + 2 * LANES)
        mixed_ref[1, :, lanes] = (own_ref[:, here] + back_ref[:, here].astype(F32)).astype(BF16)


def unproject(own, back, cosine, sine):
    rows, width = own.shape[0], own.shape[1] // 2
    tile = min(256, rows)
    return pl.pallas_call(
        unproject_kernel,
        grid=(rows // tile,),
        in_specs=[
            pl.BlockSpec((tile, 2 * width), lambda i: (i, 0)),
            pl.BlockSpec((tile, 2 * width), lambda i: (i, 0)),
            pl.BlockSpec((tile, LANES), lambda i: (i, 0)),
            pl.BlockSpec((tile, LANES), lambda i: (i, 0)),
        ],
        out_specs=pl.BlockSpec((2, tile, width), lambda i: (0, i, 0)),
        out_shape=jax.ShapeDtypeStruct((2, rows, width), BF16),
        name="unproject",
    )(own, back, cosine, sine)


def norm_forward(stream, gain_row, shift_row):
    average = jnp.mean(stream, axis=-1, keepdims=True)
    centred = stream - average
    variance = jnp.mean(centred * centred, axis=-1, keepdims=True)
    reciprocal = lax.rsqrt(variance + EPSILON)
    scaled = centred * reciprocal
    return (scaled * gain_row + shift_row, scaled, reciprocal)


def norm_backward(gradient, scaled, reciprocal, gain_row):
    weighted_grad = gradient * gain_row
    result = reciprocal * (
        weighted_grad
        - jnp.mean(weighted_grad, axis=-1, keepdims=True)
        - scaled * jnp.mean(weighted_grad * scaled, axis=-1, keepdims=True)
    )
    return (result, jnp.sum(gradient * scaled, axis=0), jnp.sum(gradient, axis=0))


def mask_rows(bias_ref, key_ref, index_ref, start_ref, row_count):
    query_index, query_start = index_ref[0], start_ref[0]
    for step in range(3):

        def fill(chunk, carry, step=step):
            key_index = key_ref[0, pl.ds(chunk * LANES, LANES), :] - step * row_count
            allowed = (key_index <= query_index) & (key_index >= query_start)
            rows = pl.ds(step * row_count + chunk * LANES, LANES)
            bias_ref[rows, :] = jnp.where(allowed, 0.0, MASKED)
            return carry

        lax.fori_loop(0, row_count // LANES, fill, 0)


def one_head(values, which):
    lane = lax.broadcasted_iota(jnp.int32, values.shape, 1)
    return jnp.where(lane // HD == which, values, jnp.zeros_like(values))


def dot_lanes(first, second):
    return lax.dot_general(first, second, (((1,), (1,)), ((), ())), preferred_element_type=F32)


def dot_rows(first, second):
    return lax.dot_general(first, second, (((0,), (0,)), ((), ())), preferred_element_type=F32)


def fold(values, operation):
    return operation(values.reshape(values.shape[0] // 8, 8, values.shape[1]), axis=0)


def attend_kernel(
    index_ref, start_ref, key_ref, query_ref, own_ref, before_ref, earlier_ref,
    turned_ref, low_ref, log_ref, bias_ref, score_ref, weight_ref,
):
    row_count = index_ref.shape[2]
    chunks = row_count // LANES

    @pl.when(pl.program_id(1) == 0)
    def _():
        mask_rows(bias_ref, key_ref, index_ref, start_ref, row_count)

    query = query_ref[...].reshape(row_count, LANES)
    blocks = (own_ref, before_ref, earlier_ref)
    for which in range(2):
        picked = one_head(query, which)
        top = jnp.full((8, row_count), MASKED, F32)
        for step in range(3):

            def score(chunk, top, step=step):
                rows = pl.ds(step * row_count + chunk * LANES, LANES)
                raw = dot_lanes(blocks[step][chunk, 0, :, :LANES], picked) + bias_ref[rows, :]
                score_ref[rows, :] = raw
                return jnp.maximum(top, fold(raw, jnp.max))

            top = lax.fori_loop(0, chunks, score, top)
        top = jnp.max(top, axis=0, keepdims=True)

        def soften(chunk, total):
            rows = pl.ds(chunk * LANES, LANES)
            weight = jnp.exp(score_ref[rows, :] - top)
            weight_ref[rows, :] = weight.astype(BF16)
            return total + fold(weight, jnp.sum)

        total = lax.fori_loop(0, 3 * chunks, soften, jnp.zeros((8, row_count), F32))
        total = jnp.sum(total, axis=0, keepdims=True)
        weighted = jnp.zeros((LANES, row_count), F32)
        for step in range(3):
            value = blocks[step][:, 0, :, LANES:].reshape(row_count, LANES)
            weighted = weighted + dot_rows(
                value, weight_ref[step * row_count : (step + 1) * row_count, :]
            )
        here = slice(which * HD, (which + 1) * HD)
        turned_ref[0, 0, here, :] = weighted[here, :] / total
        log_ref[0, 0, which : which + 1, :] = top + jnp.log(total)
    low_ref[...] = jnp.transpose(turned_ref[0, 0]).astype(BF16).reshape(low_ref.shape)


def sequence_block(width):
    return pl.BlockSpec((4, 1, LANES, width), lambda s, p: (0, s, 0, p))


def index_specs(row_count):
    return [
        pl.BlockSpec((1, 1, row_count), lambda s, p: (s, 0, 0)),
        pl.BlockSpec((1, 1, row_count), lambda s, p: (s, 0, 0)),
        pl.BlockSpec((1, row_count, 1), lambda s, p: (s, 0, 0)),
    ]


def attend(query, blocks, context):
    rows, width = query.shape
    row_count, duos = rows // 2, width // LANES
    pair_spec = pl.BlockSpec((1, 1, LANES, row_count), lambda s, p: (s, p, 0, 0))
    log_spec = pl.BlockSpec((1, 1, 2, row_count), lambda s, p: (s, p, 0, 0))
    turned, low, log_total = pl.pallas_call(
        attend_kernel,
        grid=(2, duos),
        in_specs=index_specs(row_count) + [sequence_block(LANES)] + [sequence_block(2 * LANES)] * 3,
        out_specs=[pair_spec, sequence_block(LANES), log_spec],
        out_shape=[
            jax.ShapeDtypeStruct((2, duos, LANES, row_count), F32),
            jax.ShapeDtypeStruct((4, 2, LANES, width), BF16),
            jax.ShapeDtypeStruct((2, duos, 2, row_count), F32),
        ],
        scratch_shapes=[
            pltpu.VMEM((3 * row_count, row_count), F32),
            pltpu.VMEM((3 * row_count, row_count), F32),
            pltpu.VMEM((3 * row_count, row_count), BF16),
        ],
        name="attend",
    )(*context, query.reshape(4, 2, LANES, width), *blocks)
    return turned, low.reshape(rows, width), log_total


def attend_back_kernel(
    index_ref, start_ref, key_ref, query_ref, own_ref, before_ref, earlier_ref,
    grad_ref, turned_ref, log_ref,
    query_out, own_out, before_out, earlier_out, bias_ref, score_ref,
):
    row_count = index_ref.shape[2]
    chunks = row_count // LANES

    @pl.when(pl.program_id(1) == 0)
    def _():
        mask_rows(bias_ref, key_ref, index_ref, start_ref, row_count)

    query = query_ref[...].reshape(row_count, LANES)
    grad = grad_ref[...].reshape(row_count, LANES)
    product = jnp.transpose(grad.astype(F32)) * turned_ref[0, 0]
    delta = [
        jnp.sum(product[which * HD : (which + 1) * HD], axis=0, keepdims=True)
        for which in range(2)
    ]
    queries = [one_head(query, which) for which in range(2)]
    grads = [one_head(grad, which) for which in range(2)]
    blocks = (own_ref, before_ref, earlier_ref)
    outs = (own_out, before_out, earlier_out)
    for step in range(3):

        def back(chunk, carry, step=step):
            rows = pl.ds(step * row_count + chunk * LANES, LANES)
            key = blocks[step][chunk, 0, :, :LANES]
            value = blocks[step][chunk, 0, :, LANES:]
            grad_key = jnp.zeros((LANES, LANES), F32)
            grad_value = jnp.zeros((LANES, LANES), F32)
            for which in range(2):
                raw = dot_lanes(key, queries[which]) + bias_ref[rows, :]
                weight = jnp.exp(raw - log_ref[0, 0, which : which + 1, :])
                grad_weight = dot_lanes(value, grads[which])
                grad_score = (weight * (grad_weight - delta[which])).astype(BF16)
                score_ref[which, rows, :] = grad_score
                grad_key = grad_key + jnp.dot(
                    grad_score, queries[which], preferred_element_type=F32
                )
                grad_value = grad_value + jnp.dot(
                    weight.astype(BF16), grads[which], preferred_element_type=F32
                )
            outs[step][chunk, 0, :, :LANES] = grad_key.astype(outs[step].dtype)
            outs[step][chunk, 0, :, LANES:] = grad_value.astype(outs[step].dtype)
            return carry

        lax.fori_loop(0, chunks, back, 0)
    parts = []
    for which in range(2):
        turned = jnp.zeros((LANES, row_count), F32)
        for step in range(3):
            key = blocks[step][:, 0, :, :LANES].reshape(row_count, LANES)
            turned = turned + dot_rows(
                key, score_ref[which, step * row_count : (step + 1) * row_count, :]
            )
        parts.append(turned[which * HD : (which + 1) * HD])
    turned = jnp.concatenate(parts, 0) * HD ** (-0.5)
    query_out[...] = jnp.transpose(turned).astype(BF16).reshape(query_out.shape)


def attend_backward(query, blocks, grad_heads, turned, log_total, context):
    rows, width = query.shape
    row_count, duos = rows // 2, width // LANES
    pair_spec = pl.BlockSpec((1, 1, LANES, row_count), lambda s, p: (s, p, 0, 0))
    log_spec = pl.BlockSpec((1, 1, 2, row_count), lambda s, p: (s, p, 0, 0))
    wide = (4, 2, LANES, 2 * width)
    grad_query, own, before, earlier = pl.pallas_call(
        attend_back_kernel,
        grid=(2, duos),
        in_specs=index_specs(row_count)
        + [sequence_block(LANES)]
        + [sequence_block(2 * LANES)] * 3
        + [sequence_block(LANES), pair_spec, log_spec],
        out_specs=[sequence_block(LANES)] + [sequence_block(2 * LANES)] * 3,
        out_shape=[
            jax.ShapeDtypeStruct((4, 2, LANES, width), BF16),
            jax.ShapeDtypeStruct(wide, F32),
            jax.ShapeDtypeStruct(wide, F32),
            jax.ShapeDtypeStruct(wide, BF16),
        ],
        scratch_shapes=[
            pltpu.VMEM((3 * row_count, row_count), F32),
            pltpu.VMEM((2, 3 * row_count, row_count), BF16),
        ],
        name="attend_back",
    )(
        *context, query.reshape(4, 2, LANES, width), *blocks,
        grad_heads.reshape(4, 2, LANES, width), turned, log_total,
    )
    flat = (rows, 2 * width)
    return (
        grad_query.reshape(rows, width),
        own.reshape(flat),
        before.reshape(flat),
        earlier.reshape(flat),
    )


def own_half(values, axis, size, pair):
    start = pair * (values.shape[axis] - size)
    return lax.dynamic_slice_in_dim(values, start, size, axis)


def weight_parts(layer, pair):
    w_qkv, b_qkv, w_out, w_gate_up, w_down = layer
    units = w_down.shape[0]
    columns = w_out.shape[0] // 2
    unit_count = -(-(units // 2) // LANES) * LANES
    down_part = own_half(w_down, 0, unit_count, pair)
    shared = 2 * unit_count - units
    if shared:
        repeated = (jnp.arange(unit_count) < shared)[:, None] & (pair == 1)
        down_part = jnp.where(repeated, jnp.zeros_like(down_part), down_part)
    return [
        own_half(w_qkv, 2, columns, pair),
        b_qkv,
        jnp.concatenate([own_half(w_out, 0, columns, pair), down_part], 0),
        own_half(w_gate_up, 2, unit_count, pair),
    ]


def whole(part):
    return lax.all_gather(part, "fsdp", axis=1, tiled=True)


def after(value, *others):
    return lax.optimization_barrier((value, *others))


def forward_layer(stream, parts, later, gain_rows, shift_rows, context):
    w_qkv, b_qkv, w_rows, w_gate_up = parts
    w_qkv, w_rows = whole(w_qkv), whole(w_rows)
    w_out, w_down = w_rows[: w_qkv.shape[2]], w_rows[w_qkv.shape[2] :]
    attention_context, cosine, sine_table = context
    heads = b_qkv.shape[1]
    normed, scaled_one, recip_one = norm_forward(stream, gain_rows[0], shift_rows[0])
    first_in = gather_rows(normed.astype(BF16))
    rows = first_in.shape[0]
    mixed = jnp.einsum("td,cde->cte", first_in, w_qkv, preferred_element_type=F32)
    bias = b_qkv.astype(F32).reshape(3, 1, heads * HD)
    query, packed = project(mixed, bias, cosine, sine_table)
    before = shift_fsdp(packed, 1)
    earlier = shift_fsdp(before, 1)
    earlier, w_gate_up, *later = after(earlier, w_gate_up, *later)
    w_gate_up = whole(w_gate_up)
    blocks = [part.reshape(4, 2, rows // 8, 2 * heads * HD) for part in (packed, before, earlier)]
    turned, att_low, log_total = attend(query, blocks, attention_context)
    stream_h = stream + scatter_rows(
        jnp.dot(att_low, w_out, preferred_element_type=F32).astype(BF16)
    )
    normed_two, scaled_two, recip_two = norm_forward(stream_h, gain_rows[1], shift_rows[1])
    second_in = gather_rows(normed_two.astype(BF16))
    gate_up = jnp.einsum("td,cdf->ctf", second_in, w_gate_up, preferred_element_type=F32)
    activated = (jax.nn.silu(gate_up[0]) * gate_up[1]).astype(BF16)
    result = stream_h + scatter_rows(
        jnp.dot(activated, w_down, preferred_element_type=F32).astype(BF16)
    )
    stored = (
        scaled_one,
        recip_one,
        first_in,
        query,
        blocks,
        turned,
        log_total,
        att_low,
        scaled_two,
        recip_two,
        second_in,
        gate_up,
        activated,
    )
    return (result, (w_qkv, b_qkv, w_out, w_gate_up, w_down), stored, later)


def scatter_weight(gradient, axis):
    return lax.psum_scatter(gradient.astype(BF16), "fsdp", scatter_dimension=axis, tiled=True)


def other_pairs(shard):
    count = lax.axis_size("replica")
    pair = pair_size()
    total = shard.astype(F32)
    for step in range(pair, count, pair):
        total = total + lax.ppermute(
            shard, "replica", [(i, (i + step) % count) for i in range(count)]
        ).astype(F32)
    return total.astype(BF16)


def sum_over(values, axis):
    count = lax.axis_size(axis)
    bit = 1
    while bit < count:
        values = values + lax.ppermute(values, axis, [(i, i ^ bit) for i in range(count)])
        bit *= 2
    return values


def place_lanes_kernel(pair_ref, mine_ref, theirs_ref, *rest):
    out_ref = rest[-1]
    size = mine_ref.shape[-1]
    extra = 2 * size - out_ref.shape[-1]

    def write(first, second):
        out_ref[0, 0, :, :size] = first[0].astype(F32)
        out_ref[0, 0, :, size:] = second[0, :, extra:].astype(F32)

    @pl.when(pair_ref[0] == 0)
    def _():
        write(mine_ref, theirs_ref)

    @pl.when(pair_ref[0] != 0)
    def _():
        write(theirs_ref, mine_ref)


def place_rows_kernel(pair_ref, mine_ref, theirs_ref, *rest):
    out_ref = rest[-1]
    size = mine_ref.shape[0]
    extra = 2 * size - out_ref.shape[1]

    def write(first, second):
        out_ref[0, :size] = first[...].astype(F32)
        out_ref[0, size:] = second[extra:].astype(F32)

    @pl.when(pair_ref[0] == 0)
    def _():
        write(mine_ref, theirs_ref)

    @pl.when(pair_ref[0] != 0)
    def _():
        write(theirs_ref, mine_ref)


def place_turned_kernel(pair_ref, mine_ref, theirs_ref, *rest):
    out_ref = rest[-1]
    size = mine_ref.shape[0]

    def write(first, second):
        out_ref[0, 0, :, :size] = jnp.transpose(first[...].astype(F32))
        out_ref[0, 0, :, size:] = jnp.transpose(second[...].astype(F32))

    @pl.when(pair_ref[0] == 0)
    def _():
        write(mine_ref, theirs_ref)

    @pl.when(pair_ref[0] != 0)
    def _():
        write(theirs_ref, mine_ref)


def exchange(shard):
    mine = other_pairs(shard)
    return mine, swap_replica(mine)


def place(both, layer, layers, buffer, pair, first=0, parts=None, units=None, turned=False):
    mine, theirs = both
    pair = pair.astype(jnp.int32).reshape(1)
    if parts is None:
        total = units
        size, width = min(mine.shape[0], -(-(total // 2) // LANES) * LANES), mine.shape[1]
        tile = LANES
        grid = (width // tile,)
        in_spec = pl.BlockSpec((size, tile), lambda i, p: (0, i))
        out_spec = pl.BlockSpec((1, total, tile), lambda i, p: (layer, 0, i))
        shape = (layers, total, width)
        kernel = place_rows_kernel
    elif turned:
        size, width = mine.shape[0] // 2, mine.shape[1]
        tile = min(256, width)
        grid = (width // tile,)
        in_spec = pl.BlockSpec((size, tile), lambda i, p: (1, i))
        out_spec = pl.BlockSpec((1, 1, tile, units), lambda i, p: (layer, first, i, 0))
        shape = (layers, parts, width, units)
        kernel = place_turned_kernel
    else:
        count, rows, size = mine.shape
        tile = min(256, rows)
        grid = (count, rows // tile)
        in_spec = pl.BlockSpec((1, tile, size), lambda c, i, p: (c, i, 0))
        out_spec = pl.BlockSpec((1, 1, tile, units), lambda c, i, p: (layer, c + first, i, 0))
        shape = (layers, parts, rows, units)
        kernel = place_lanes_kernel
    operands = [pair, mine, theirs]
    in_specs = [in_spec, in_spec]
    aliases = {}
    if buffer is not None:
        operands.append(buffer)
        in_specs.append(pl.BlockSpec(memory_space=pl.ANY))
        aliases = {3: 0}
    return pl.pallas_call(
        kernel,
        grid_spec=pltpu.PrefetchScalarGridSpec(
            num_scalar_prefetch=1, grid=grid, in_specs=in_specs, out_specs=out_spec
        ),
        out_shape=jax.ShapeDtypeStruct(shape, F32),
        input_output_aliases=aliases,
        name="place",
    )(*operands)


def backward_layer(grad_stream, weights, gain_rows, stored, context, pending):
    w_qkv, b_qkv, w_out, w_gate_up, w_down = weights
    attention_context, cosine, sine_table = context
    (
        scaled_one,
        recip_one,
        first_in,
        query,
        blocks,
        turned,
        log_total,
        att_low,
        scaled_two,
        recip_two,
        second_in,
        gate_up,
        activated,
    ) = stored
    heads = b_qkv.shape[1]
    grad_out = gather_rows(grad_stream.astype(BF16))
    rows = grad_out.shape[0]
    grad_act = jnp.einsum("td,fd->tf", grad_out, w_down, preferred_element_type=F32)
    gate_part, up_part = gate_up[0], gate_up[1]
    sigmoid_gate = jax.nn.sigmoid(gate_part)
    grad_gate = grad_act * up_part * sigmoid_gate * (1.0 + gate_part * (1.0 - sigmoid_gate))
    grad_up = grad_act * gate_part * sigmoid_gate
    grad_mix_two = jnp.stack([grad_gate, grad_up]).astype(BF16)
    back = jnp.einsum("ctf,cdf->td", grad_mix_two, w_gate_up, preferred_element_type=F32)
    grad_norm_two = scatter_rows(back.astype(BF16))
    if pending:
        grad_norm_two = after(grad_norm_two, *pending)[0]
    grad_down = exchange(
        scatter_weight(
            jnp.einsum("tf,td->fd", activated, grad_out, preferred_element_type=F32), 1
        )
    )
    grad_gate_up = exchange(
        scatter_weight(
            jnp.einsum("td,ctf->cdf", second_in, grad_mix_two, preferred_element_type=F32), 1
        )
    )
    back_two, gain_grad_two, shift_grad_two = norm_backward(
        grad_norm_two, scaled_two, recip_two, gain_rows[1]
    )
    grad_hidden = grad_stream + back_two
    grad_att = gather_rows(grad_hidden.astype(BF16))
    grad_heads = jnp.einsum("td,ed->te", grad_att, w_out, preferred_element_type=F32)
    grad_heads = grad_heads.astype(BF16)
    grad_wout = jnp.einsum("te,td->ed", att_low, grad_att, preferred_element_type=F32)
    grad_query, own, before, earlier = attend_backward(
        query, blocks, grad_heads, turned, log_total, attention_context
    )
    query_mixed = unproject_query(grad_query, cosine, sine_table)
    grad_wquery = jnp.einsum("te,td->ed", query_mixed, first_in, preferred_element_type=F32)
    grad_rows = jnp.concatenate([grad_wout.astype(BF16), grad_wquery.astype(BF16)], 0)
    earlier, before, grad_rows = after(
        earlier, before, grad_rows, grad_down[1], grad_gate_up[0]
    )[:3]
    grad_rows = exchange(scatter_weight(grad_rows, 1))
    returned = shift_fsdp(earlier, -1)
    returned = shift_fsdp((before + returned.astype(F32)).astype(BF16), -1)
    returned = after(returned, grad_gate_up[1], grad_rows[0])[0]
    grad_mixed = unproject(own, returned, cosine, sine_table)
    back = jnp.einsum("te,de->td", query_mixed, w_qkv[0], preferred_element_type=F32)
    back = back + jnp.einsum("cte,cde->td", grad_mixed, w_qkv[1:], preferred_element_type=F32)
    grad_wkv = jnp.einsum("td,cte->cde", first_in, grad_mixed, preferred_element_type=F32)
    back, grad_wkv = after(back.astype(BF16), grad_wkv.astype(BF16))
    grad_wkv = exchange(scatter_weight(grad_wkv, 1))
    grad_norm_one = scatter_rows(back)
    grad_bias = jnp.concatenate(
        [
            jnp.sum(query_mixed, axis=0, dtype=F32, keepdims=True),
            jnp.sum(grad_mixed, axis=1, dtype=F32),
        ],
        0,
    )
    back_one, gain_grad_one, shift_grad_one = norm_backward(
        grad_norm_one, scaled_one, recip_one, gain_rows[0]
    )
    grad_input = grad_hidden + back_one
    norm_grads = jnp.stack([gain_grad_one, gain_grad_two, shift_grad_one, shift_grad_two])
    return (
        grad_input,
        (grad_gate_up, grad_down, grad_rows, grad_wkv),
        norm_grads,
        grad_bias,
    )


def body(tokens, segments, w_qkv, b_qkv, w_out, w_gate_up, w_down, ln_gain, ln_bias, cotangent):
    layers = w_qkv.shape[0]
    row_count = tokens.shape[1]
    tensor_count = lax.axis_size("tensor")
    group_rows = row_count * tensor_count
    replica = lax.axis_index("replica")
    pair = replica % 2
    block = lax.axis_index("fsdp")
    own = lax.axis_index("tensor")

    small = jnp.concatenate([ln_gain.reshape(-1), ln_bias.reshape(-1), b_qkv.reshape(-1)])
    small = lax.all_gather(small.reshape(-1, LANES), ("fsdp", "tensor"), axis=0)
    blocks = lax.axis_size("fsdp")
    norm_size, shift_size = ln_gain.size, 2 * ln_gain.size
    small = small.reshape(blocks, tensor_count, -1)

    def whole_rows(flat):
        flat = flat.reshape(blocks * tensor_count, layers, 2, ln_gain.shape[2])
        return jnp.transpose(flat, (1, 2, 0, 3)).reshape(layers, 2, -1).astype(F32)

    gain_all = whole_rows(small[:, :, :norm_size])
    shift_all = whole_rows(small[:, :, norm_size:shift_size])
    biases = lax.dynamic_index_in_dim(small[:, :, shift_size:], own, 1, keepdims=False)
    biases = biases.reshape(blocks, layers, 3, b_qkv.shape[2], b_qkv.shape[3])
    biases = jnp.transpose(biases, (1, 2, 3, 0, 4)).reshape(layers, 3, b_qkv.shape[2], -1)
    biases = own_half(biases, 2, b_qkv.shape[2] // 2, pair)

    both_segments = jnp.concatenate([segments, swap_replica(segments)], 0)
    starts = lax.dynamic_slice_in_dim(
        segment_starts(both_segments), block * group_rows, group_rows, 1
    )
    index = block * group_rows + jnp.arange(group_rows, dtype=jnp.int32)
    index = jnp.broadcast_to(index[None, :], starts.shape)
    shape = (2, tensor_count, 2, row_count // 2)
    row_start = order_rows(starts.reshape(shape), own)
    row_index = order_rows(index.reshape(shape), own)
    cosine, sine_table = rotary_tables(row_index - row_start)

    def split(flat):
        return jnp.transpose(flat.reshape(4, 2, -1), (1, 0, 2)).reshape(2, -1)

    query_index = split(row_index)
    attention_context = (
        query_index[:, None, :],
        split(row_start)[:, None, :],
        query_index[:, :, None],
    )
    context = (attention_context, cosine, sine_table)

    stream = tokens[0].astype(F32)
    kept = []
    parts = [
        weight_parts(
            (w_qkv[layer], biases[layer], w_out[layer], w_gate_up[layer], w_down[layer]), pair
        )
        for layer in range(layers)
    ]
    for layer in range(layers):
        later = [part for following in parts[layer + 1 :] for part in (following[0], *following[2:])]
        stream, weights, stored, later = forward_layer(
            stream, parts[layer], later, gain_all[layer], shift_all[layer], context
        )
        for i, following in enumerate(parts[layer + 1 :]):
            following[0], following[2:] = later[3 * i], later[3 * i + 1 : 3 * i + 3]
        kept.append((weights, stored))
    output = stream.astype(BF16)[None]

    grad_stream = cotangent[0].astype(F32)
    norm_parts = [None] * layers
    bias_parts = [None] * layers
    buffers = [None] * 4
    columns, units = w_qkv.shape[3], w_down.shape[1]

    shards = [None] * layers
    pending = ()
    for layer in reversed(range(layers)):
        weights, stored = kept[layer]
        grad_stream, shards[layer], norm_parts[layer], bias_parts[layer] = backward_layer(
            grad_stream, weights, gain_all[layer], stored, context, pending
        )
        pending = (shards[layer][2][1], shards[layer][3][1])
    gated = [part for layer in range(layers) for both in shards[layer][:2] for part in both]
    grad_stream, *gated = after(grad_stream, *gated)
    for layer in reversed(range(layers)):
        wide, down = gated[4 * layer : 4 * layer + 2], gated[4 * layer + 2 : 4 * layer + 4]
        rows, late = shards[layer][2:]
        buffers[2] = place(wide, layer, layers, buffers[2], pair, parts=2, units=units)
        buffers[3] = place(down, layer, layers, buffers[3], pair, units=units)
        buffers[1] = place(rows, layer, layers, buffers[1], pair, units=columns)
        buffers[0] = place(
            rows, layer, layers, buffers[0], pair, parts=3, units=columns, turned=True
        )
        buffers[0] = place(
            late, layer, layers, buffers[0], pair, first=1, parts=3, units=columns
        )

    norm_flat = jnp.stack(norm_parts).reshape(-1)
    bias_flat = jnp.stack(bias_parts).reshape(-1)
    norm_count = norm_flat.shape[0]
    summed = sum_over(jnp.concatenate([norm_flat, bias_flat]).reshape(-1, LANES), "fsdp")
    bias_mine = summed[norm_count // LANES :]
    for bit in range(1, (lax.axis_size("replica") - 1).bit_length()):
        bias_mine = bias_mine + lax.ppermute(
            bias_mine, "replica", [(i, i ^ (1 << bit)) for i in range(lax.axis_size("replica"))]
        )
    bias_other = swap_replica(bias_mine)
    summed = sum_over(summed[: norm_count // LANES], "tensor")
    width = stream.shape[1]
    norm_sum = sum_over(summed, "replica").reshape(layers, 4, width)
    slice_width = ln_gain.shape[2]
    norm_sum = lax.dynamic_slice_in_dim(
        norm_sum, (block * tensor_count + own) * slice_width, slice_width, 2
    )
    grad_gain, grad_shift = norm_sum[:, :2], norm_sum[:, 2:]
    shape = (layers, 3, b_qkv.shape[2] // 2, HD)
    bias_mine, bias_other = bias_mine.reshape(shape), bias_other.reshape(shape)
    bias_sum = jnp.concatenate(
        [
            jnp.where(pair == 0, bias_mine, bias_other),
            jnp.where(pair == 0, bias_other, bias_mine),
        ],
        2,
    )
    bias_width = b_qkv.shape[3]
    grad_bias = lax.dynamic_slice_in_dim(bias_sum, block * bias_width, bias_width, 3)

    return (
        output,
        grad_stream[None],
        buffers[0],
        grad_bias,
        buffers[1],
        buffers[2],
        buffers[3],
        grad_gain,
        grad_shift,
    )


def solution(mesh):
    return jax.shard_map(
        body,
        mesh=mesh,
        in_specs=(
            P("replica", ("fsdp", "tensor"), None),
            P("replica", None),
            P(None, None, "fsdp", "tensor"),
            P(None, None, "tensor", "fsdp"),
            P(None, "tensor", "fsdp"),
            P(None, None, "fsdp", "tensor"),
            P(None, "tensor", "fsdp"),
            P(None, None, ("fsdp", "tensor")),
            P(None, None, ("fsdp", "tensor")),
            P("replica", ("fsdp", "tensor"), None),
        ),
        out_specs=(
            P("replica", ("fsdp", "tensor"), None),
            P("replica", ("fsdp", "tensor"), None),
            P(None, None, "fsdp", "tensor"),
            P(None, None, "tensor", "fsdp"),
            P(None, "tensor", "fsdp"),
            P(None, None, "fsdp", "tensor"),
            P(None, "tensor", "fsdp"),
            P(None, None, ("fsdp", "tensor")),
            P(None, None, ("fsdp", "tensor")),
        ),
        check_vma=False,
    )
```
